512 devices in a mesh: dp: 32 (over z, x), tensor: 16 (over y, core).
Axes of the slice: x: 4, y: 8, z: 8, core: 2. Of those that a mesh axis runs over, the one named last changes fastest.
Arguments:
- activations: bfloat16 [16384, 4096], P('dp', 'tensor'), may hold values from -6 to 6
- base_weight: bfloat16 [4096, 4096], P('tensor'), may hold values from -8.4375 to 8.4375
- adapter_in: float32 [4096, 64], P('tensor'), may hold values from -0.09375 to 0.09375
- adapter_out: float32 [64, 4096], replicated, may hold values from -0.75 to 0.75
- magnitude: float32 [4096], replicated, may hold values from 0.5 to 2
- cotangent: bfloat16 [16384, 4096], P(('dp', 'tensor')), may hold values from -1.5 to 1.5
Outputs:
- output: bfloat16 [16384, 4096], P(('dp', 'tensor'))
- grad_act: bfloat16 [16384, 4096], P('dp', 'tensor')
- grad_in: float32 [4096, 64], P('tensor')
- grad_out: float32 [64, 4096], replicated
- grad_mag: float32 [4096], replicated
The draws below stay inside these ranges and needn't reach their ends.
All inputs are finite; a program needn't handle non-finite values.
Results may differ from the reference program's by a relative error of at most 0.0057.
Values may be sent and summed in bfloat16 or wider, within the bound.
No kernel may reach another device: no remote copies, remote signals or barrier semaphores. Data moves between devices by JAX's collectives and lax.ppermute only.
A program may use at most 128 MiB of HBM per device.

```python
import math
import jax
import jax.numpy as jnp
from jax import lax

IN = 4096
OUT = 4096
R = 64
TOKENS = 16384


def draw_base_weight(key, part):
    keys = jax.random.split(jax.random.fold_in(key, 11), 3)
    noise = jnp.clip(jax.random.normal(keys[0], (IN, OUT), jnp.float32), -6.0, 6.0)
    ramp = jnp.exp(jnp.log(3.0) * jnp.arange(IN, dtype=jnp.float32) / IN)[:, None]
    row_scale = jnp.exp(jax.random.uniform(keys[1], (IN, 1), jnp.float32) * jnp.log(10.0)) * ramp
    col_scale = jnp.exp(jax.random.uniform(keys[2], (1, OUT), jnp.float32) * jnp.log(10.0))
    return (noise * row_scale * col_scale / (10.0 * jnp.sqrt(jnp.float32(IN)))).astype(jnp.bfloat16)


def block_levels(rng, extent, cuts, low, high):
    loudness, own = 1.0, jax.random.fold_in(rng, 6)
    for axis_at, blocks in cuts:
        draws = jnp.exp(jax.random.uniform(jax.random.fold_in(own, axis_at), (blocks,), jnp.float32, low / len(cuts), high / len(cuts)))
        loudness = loudness * jnp.repeat(draws, extent[axis_at] // blocks).reshape([-1 if axis == axis_at else 1 for axis in range(len(extent))])
    return loudness


def gaussian(rng, shape, width, limit, cuts=(), kind=jnp.bfloat16):
    level = block_levels(rng, shape, cuts, -0.22, 0.18) if cuts else 1.0
    values = jax.random.normal(rng, shape, jnp.float32) * width * level
    return jnp.minimum(jnp.maximum(values, -limit), limit).astype(kind)


def setup_inputs(seed: int = 0) -> dict:
    key_list = jax.random.split(jax.random.key(seed), 7)
    return {
        "activations": gaussian(key_list[0], (TOKENS, IN), 1.0, 6.0, ((0, 32), (1, 16))),
        "base_weight": draw_base_weight(jax.random.fold_in(key_list[6], 71), 0),
        "adapter_in": gaussian(key_list[2], (IN, R), IN ** -0.5, 0.09375, ((0, 16),), jnp.float32),
        "adapter_out": gaussian(key_list[3], (R, OUT), R ** -0.5, 0.75, (), jnp.float32),
        "magnitude": jnp.clip(jnp.exp(jax.random.uniform(key_list[4], (OUT,), jnp.float32, math.log(0.5), math.log(2.0))), 0.5, 2.0),
        "cotangent": gaussian(key_list[5], (TOKENS, OUT), 0.25, 1.5, ((0, 512),)),
    }


epsilon = 1e-06

def reference(activations, base_weight, adapter_in, adapter_out, magnitude, cotangent):
    highest = lax.Precision.HIGHEST
    merged = base_weight.astype(jnp.float32) + jnp.dot(adapter_in, adapter_out, precision=highest)
    col_norm = jnp.sqrt(lax.optimization_barrier(jnp.sum(merged * merged, axis=0)) + epsilon)
    col_scale = magnitude / col_norm
    merged_low = merged.astype(jnp.bfloat16)
    summed = jnp.dot(activations, merged_low, preferred_element_type=jnp.float32)
    output = (summed * col_scale).astype(jnp.bfloat16)
    cot_float = cotangent.astype(jnp.float32)
    grad_scaled = (cot_float * col_scale).astype(jnp.bfloat16)
    grad_act = lax.dot_general(grad_scaled, merged_low, (((1,), (1,)), ((), ())), preferred_element_type=jnp.float32).astype(jnp.bfloat16)
    grad_mag = lax.optimization_barrier(jnp.sum(cot_float * summed, axis=0)) / col_norm
    norm_coeff = -grad_mag * magnitude / (col_norm * col_norm)
    grad_dir = lax.dot_general(activations, grad_scaled, (((0,), (0,)), ((), ())), preferred_element_type=jnp.float32)
    grad_dir = grad_dir + merged * norm_coeff
    grad_in = jnp.dot(grad_dir, adapter_out.T, precision=highest)
    grad_out = jnp.dot(adapter_in.T, grad_dir, precision=highest)
    return (output, grad_act, grad_in, grad_out, grad_mag)
```

```python
import jax
import jax.numpy as jnp
from jax import lax
from jax.experimental import pallas as pl
from jax.experimental.pallas import tpu as pltpu
from jax.sharding import Mesh, PartitionSpec as P


epsilon = 1e-06
F32, BF16 = jnp.float32, jnp.bfloat16
REPLICA = ("z", "x")
TENSOR = ("y", "core")
TILE = 512


def split(value):
    high = value.astype(BF16)
    return high, (value - high.astype(F32)).astype(BF16)


def contract(left, right, dims):
    return lax.dot_general(left, right, ((dims[:1], dims[1:]), ((), ())), preferred_element_type=F32)


def merge_kernel(base_ref, wide_ref, pick_ref, out_ref, zt, low_ref, first_ref):
    step = pl.program_id(0)
    ah, al = split(out_ref[...])
    low = contract(wide_ref[...], jnp.concatenate([ah, al, ah, al], 0), (1, 0))
    merged = base_ref[...].astype(F32) + low
    squares = jnp.sum(merged * merged, axis=0, keepdims=True)
    rounded = merged.astype(BF16)

    low_ref[...] = rounded
    picked = contract(pick_ref[...], rounded, (1, 0))
    picked = picked[0:8] + picked[8:16]
    ranks = zt[pl.ds(pl.multiple_of(step * 16, 16), 16), :]
    for k in range(4):
        for q in range(4):
            first_ref[k, 4 * q : 4 * q + 4, :] = ranks[4 * k : 4 * k + 4, 128 * q : 128 * q + 128]
        for r in range(2):
            span = slice(256 * k + 128 * r, 256 * k + 128 * r + 128)
            first_ref[k, 16 + r : 17 + r, :] = squares[:, span]
            first_ref[k, 18 + r : 19 + r, :] = picked[0:1, span]
            first_ref[k, 20 + r : 21 + r, :] = picked[1:2, span]
        first_ref[k, 22:24, :] = jnp.zeros((2, 128), F32)


def merge(base, wide, pick, adapter_out, zt):
    rows, cols = base.shape
    tokens = zt.shape[1]
    steps = cols // 1024
    tile = lambda i: (0, i)
    whole = lambda i: (0, 0)
    return pl.pallas_call(
        merge_kernel,
        out_shape=(
            jax.ShapeDtypeStruct((rows, cols), BF16),
            jax.ShapeDtypeStruct((16, 24, 128), F32),
        ),
        grid_spec=pltpu.PrefetchScalarGridSpec(
            num_scalar_prefetch=0,
            grid=(steps,),
            in_specs=[
                pl.BlockSpec((rows, 1024), tile),
                pl.BlockSpec((rows, 256), whole),
                pl.BlockSpec((16, rows), whole),
                pl.BlockSpec((64, 1024), tile),
                pl.BlockSpec((64, tokens), whole),
            ],
            out_specs=(
                pl.BlockSpec((rows, 1024), tile),
                pl.BlockSpec((4, 24, 128), lambda i: (i, 0, 0)),
            ),
        ),
        cost_estimate=pl.CostEstimate(flops=1400000000, bytes_accessed=7000000, transcendentals=0),
        name="merge",
    )(base, wide, pick, adapter_out, zt)


def forward_kernel(at_ref, a_ref, b_ref, wa_ref, wb_ref, r4_ref, r3_ref, r2_ref, r1_ref, r0_ref, acts):
    @pl.when(pl.program_id(0) == 0)
    def _():
        for k in range(8):
            rows = pl.ds(pl.multiple_of(at_ref[17 + k] * 32, 32), 32)
            acts[32 * k : 32 * k + 32, :256] = a_ref[rows, :]
            acts[32 * k : 32 * k + 32, 256:] = b_ref[rows, :]

    part = contract(acts[...], jnp.concatenate([wa_ref[...], wb_ref[...]], 0), (1, 0))
    r4_ref[...] = part[0:32].astype(BF16)
    r3_ref[...] = part[32:96]
    r2_ref[...] = part[96:160]
    r1_ref[...] = part[160:224]
    r0_ref[...] = part[224:256]


def forward(at, act_own, act_peer, w_own, w_peer):
    tokens, feats = act_own.shape
    cols = w_own.shape[1]
    whole = pl.BlockSpec((tokens, feats), lambda i, c: (0, 0))
    tile = lambda rows: pl.BlockSpec((rows, 1024), lambda i, c: (0, i))
    rows = (32, 64, 64, 64, 32)
    kinds = (BF16, F32, F32, F32, F32)
    return pl.pallas_call(
        forward_kernel,
        out_shape=tuple(jax.ShapeDtypeStruct((r, cols), k) for r, k in zip(rows, kinds)),
        grid_spec=pltpu.PrefetchScalarGridSpec(
            num_scalar_prefetch=1,
            grid=(cols // 1024,),
            in_specs=[whole, whole, tile(feats), tile(feats)],
            out_specs=tuple(tile(r) for r in rows),
            scratch_shapes=[pltpu.VMEM((256, 512), BF16)],
        ),
        cost_estimate=pl.CostEstimate(flops=2 * tokens * feats * cols, bytes_accessed=5000000, transcendentals=0),
        name="forward",
    )(at, act_own, act_peer, w_own, w_peer)


def backward_kernel(
    at_ref, block_ref, hop1_ref, hop2_ref, hop3_ref, hop4_ref, cross_ref, scale_ref,
    wo_ref, wp_ref, ato_ref, atp_ref, second_ref, out_ref,
    gao_ref, gap_ref, in_ref, gm_ref, p_ref, cots, sum_own, sum_peer, sum_y, zt,
):
    step = pl.program_id(0)

    @pl.when(step == 0)
    def _():
        for m in range(16):
            for q in range(4):
                zt[4 * m : 4 * m + 4, 128 * q : 128 * q + 128] = second_ref[m, 4 * q : 4 * q + 4, :]

    parts = [block_ref, hop1_ref, hop2_ref, hop3_ref, hop4_ref]
    parts = [(part, r) for part in parts for r in (0, 32)] + [(cross_ref, r) for r in range(0, 192, 32)]
    for k, (part, r) in enumerate(parts):
        cots[pl.ds(pl.multiple_of(at_ref[1 + k] * 32, 32), 32), :] = part[r : r + 32, :]
    cot = cots[...]
    scaled = (cot.astype(F32) * scale_ref[...]).astype(BF16)
    w_own, w_peer = wo_ref[...], wp_ref[...]
    slope = jnp.sum(contract(ato_ref[...], cot, (1, 0)) * w_own.astype(F32), axis=0, keepdims=True)
    gm_ref[...] = slope + jnp.sum(contract(atp_ref[...], cot, (1, 0)) * w_peer.astype(F32), axis=0, keepdims=True)
    zh, zl = split(zt[...])
    both = contract(jnp.concatenate([zh, zl], 0), scaled, (1, 0))
    p_ref[...] = (both[:64] + both[64:]).astype(BF16)
    ah, al = split(out_ref[...])
    own = contract(scaled, w_own, (1, 1))
    peer = contract(scaled, w_peer, (1, 1))
    y = contract(scaled, jnp.concatenate([ah, al], 0), (1, 1))

    @pl.when(step == 0)
    def _():
        sum_own[...] = own
        sum_peer[...] = peer
        sum_y[...] = y

    @pl.when(step > 0)
    def _():
        sum_own[...] += own
        sum_peer[...] += peer
        sum_y[...] += y

    @pl.when(step == pl.num_programs(0) - 1)
    def _():
        gao_ref[...] = sum_own[...]
        gap_ref[...] = sum_peer[...].astype(BF16)
        pair = jnp.concatenate(split(sum_y[...]), 0)
        for k, ref in enumerate((ato_ref, atp_ref)):
            both = contract(jnp.concatenate([ref[...], ref[...]], 1), pair, (1, 0))
            in_ref[256 * k : 256 * k + 256, :] = (both[:, :64] + both[:, 64:]).astype(BF16)


def backward(at, block, hops, hop4, crossed, scale, w_own, w_peer, at_own, at_peer, second, adapter_out):
    cols = hop4.shape[1]
    feats, tokens = at_own.shape
    steps = cols // TILE
    whole = lambda i, c: (0, 0)
    tile = lambda i, c: (0, i)
    side = lambda i, c: (0, c[0] * steps + i)
    return pl.pallas_call(
        backward_kernel,
        out_shape=(
            jax.ShapeDtypeStruct((tokens, feats), F32),
            jax.ShapeDtypeStruct((tokens, feats), BF16),
            jax.ShapeDtypeStruct((2 * feats, 64), BF16),
            jax.ShapeDtypeStruct((1, cols), F32),
            jax.ShapeDtypeStruct((64, cols), BF16),
        ),
        grid_spec=pltpu.PrefetchScalarGridSpec(
            num_scalar_prefetch=1,
            grid=(steps,),
            in_specs=[pl.BlockSpec((64, TILE), side)] * 4
            + [
                pl.BlockSpec((64, TILE), tile),
                pl.BlockSpec((192, TILE), tile),
                pl.BlockSpec((1, TILE), side),
                pl.BlockSpec((feats, TILE), side),
                pl.BlockSpec((feats, TILE), side),
                pl.BlockSpec((feats, tokens), whole),
                pl.BlockSpec((feats, tokens), whole),
                pl.BlockSpec((16, 24, 128), lambda i, c: (0, 0, 0)),
                pl.BlockSpec((64, TILE), side),
            ],
            out_specs=(
                pl.BlockSpec((tokens, feats), whole),
                pl.BlockSpec((tokens, feats), whole),
                pl.BlockSpec((2 * feats, 64), whole),
                pl.BlockSpec((1, TILE), tile),
                pl.BlockSpec((64, TILE), tile),
            ),
            scratch_shapes=[
                pltpu.VMEM((tokens, TILE), BF16),
                pltpu.VMEM((tokens, feats), F32),
                pltpu.VMEM((tokens, feats), F32),
                pltpu.VMEM((tokens, 128), F32),
                pltpu.VMEM((64, tokens), F32),
            ],
        ),
        cost_estimate=pl.CostEstimate(flops=5000000000, bytes_accessed=8000000, transcendentals=0),
        name="backward",
    )(at, block, *hops, hop4, crossed, scale, w_own, w_peer, at_own, at_peer, second, adapter_out)


def finish_kernel(at_ref, wo_ref, wp_ref, a_ref, c_ref, o_ref):
    high, low = split(a_ref[...] * c_ref[...])
    pair = jnp.concatenate([high, low], 0)
    own = contract(wo_ref[...], pair, (1, 1))
    o_ref[0:256, :] = own[:, :64] + own[:, 64:]
    peer = contract(wp_ref[...], pair, (1, 1))
    o_ref[256:512, :] = peer[:, :64] + peer[:, 64:]


def finish(at, w_own, w_peer, adapter_out, coeff):
    cols = coeff.shape[1]
    side = lambda i, c: (0, c[0])
    return pl.pallas_call(
        finish_kernel,
        out_shape=jax.ShapeDtypeStruct((512, 64), F32),
        grid_spec=pltpu.PrefetchScalarGridSpec(
            num_scalar_prefetch=1,
            grid=(1,),
            in_specs=[
                pl.BlockSpec((256, cols), side),
                pl.BlockSpec((256, cols), side),
                pl.BlockSpec((64, cols), side),
                pl.BlockSpec((1, cols), lambda i, c: (0, 0)),
            ],
            out_specs=pl.BlockSpec((512, 64), lambda i, c: (0, 0)),
        ),
        cost_estimate=pl.CostEstimate(flops=600000000, bytes_accessed=3000000, transcendentals=0),
        name="finish",
    )(at, w_own, w_peer, adapter_out, coeff)


def program(activations, base_weight, adapter_in, adapter_out, magnitude, cotangent):
    core = lax.axis_index("core")
    y = lax.axis_index("y")
    replica = lax.axis_index(REPLICA)
    sides = lax.axis_size("y")
    replicas = lax.axis_size(REPLICA)
    half = adapter_out.shape[1] // 2
    hops = [(2 * s, 2 * ((s + 1) % sides)) for s in range(sides)]
    hops += [(2 * s + 1, 2 * ((s - 1) % sides) + 1) for s in range(sides)]

    def swap(value):
        return lax.ppermute(value, "core", [(0, 1), (1, 0)])

    def shift(value):
        return lax.ppermute(value, TENSOR, hops)

    def exchange(value, axes):
        return lax.all_to_all(value, axes, 0, 0)

    def spread(value, axes):
        return exchange(jnp.broadcast_to(value, (lax.axis_size(axes),) + value.shape), axes)

    mine = lambda value: lax.dynamic_slice_in_dim(value, core * half, half, 1)
    other = lambda value: lax.dynamic_slice_in_dim(value, (1 - core) * half, half, 1)

    block = jnp.concatenate([cotangent, swap(cotangent)], 0)
    hop1 = shift(block)
    hop2 = shift(hop1)
    hop3 = shift(hop2)
    sign = 1 - 2 * core
    near, far = [], []
    for k in range(5):
        chip = lax.rem(y - sign * k + sides, sides) * 2
        near += [chip + core, chip + 1 - core]
    for k in range(1, 4):
        chip = lax.rem(y + sign * k + sides, sides) * 2
        far += [chip + 1 - core, chip + core]
    rows = [lax.rem(y + sign * 4 + sides, sides) * 2 + core]
    for k in (3, 2, 1):
        chip = lax.rem(y + sign * k + sides, sides) * 2
        rows += [chip + core, chip + 1 - core]
    rows += [2 * y + core]
    at = jnp.stack([core] + near + far + rows).astype(jnp.int32)

    act_peer = swap(activations)
    high = lax.reduce_precision(adapter_in, 8, 7)
    rest = (adapter_in - high).astype(BF16)
    high = high.astype(BF16)
    wide = jnp.concatenate([high, high, rest, rest], 1)
    pair = jnp.concatenate([high.T, rest.T], 0)
    none = jnp.zeros((6, 256), BF16)
    pick = [lax.dynamic_slice_in_dim(pair, 64 * k + replica * 2, 2, 0) for k in range(2)]
    pick = jnp.concatenate([pick[0], none, pick[1], none], 0)
    at_own = activations.T
    z = contract(pair, at_own, (1, 0))
    w_own, first = merge(base_weight, wide, pick, adapter_out, z[:64] + z[64:])
    w_peer = swap(w_own)
    first = jnp.sum(exchange(first, TENSOR), axis=0)
    second = spread(first, TENSOR)
    hop4 = shift(mine(hop3))
    crossed = swap(jnp.concatenate([other(hop1), other(hop2), other(hop3)], 0))

    square_sum = second[:, 16:18].reshape(1, 2 * half)
    col_norm = jnp.sqrt(square_sum + epsilon)
    magnitude = magnitude.reshape(1, 2 * half)
    col_scale = magnitude / col_norm
    norm, size = mine(col_norm), mine(magnitude)
    q_mine = lax.dynamic_slice_in_dim(second, core * 8, 8, 0)[:, 18:22].reshape(8, 2, 256)
    q_mine = q_mine.transpose(1, 0, 2).reshape(32, 128).astype(BF16)
    q_half = spread(q_mine, REPLICA).reshape(64, half).astype(F32)

    r4, r3, r2, r1, r0 = forward(at, activations, act_peer, w_own, w_peer)
    got = shift(r4).astype(F32)
    got = shift(jnp.concatenate([r3[:32] + got, r3[32:]], 0).astype(BF16)).astype(F32)
    got = shift((r2 + got).astype(BF16)).astype(F32)
    got = shift((r1 + got).astype(BF16))
    summed = r0 + got[:32].astype(F32) + swap(got[32:]).astype(F32)
    output = (summed * col_scale).astype(BF16)

    at_peer = act_peer.T
    act_own, act_send, in_part, slope, p_part = backward(
        at, block, (hop1, hop2, hop3), hop4, crossed, col_scale, w_own, w_peer, at_own, at_peer, second, adapter_out
    )
    low = jnp.concatenate([p_part.reshape(replicas, 32, 128), in_part.reshape(replicas, 8, 128)], 1)
    low, q_half = lax.optimization_barrier((low, q_half))
    low = jnp.sum(exchange(low, REPLICA).astype(F32), axis=0).astype(BF16)
    slope = lax.psum(slope, "y")
    high = lax.reduce_precision(slope, 8, 7)
    pair = jnp.concatenate([high.reshape(16, 128), (slope - high).reshape(16, 128)], 0).astype(BF16)
    low = spread(jnp.concatenate([low, pair], 0), REPLICA)
    act_add = swap(act_send)

    slope = jnp.sum(low[:, 40:56].astype(F32) + low[:, 56:].astype(F32), axis=0).reshape(1, half)
    mag_mine = slope / norm
    coeff = -mag_mine * size / (norm * norm)
    in_sum = low[:, 32:40].reshape(512, 64).astype(F32) + finish(at, w_own, w_peer, adapter_out, coeff)
    out_mine = low[:, :32].reshape(64, half).astype(F32) + q_half * coeff
    last = swap(jnp.concatenate([out_mine, in_sum[256:].reshape(8, half), mag_mine], 0))
    grad_in = in_sum[:256] + last[64:72].reshape(256, 64)
    join = lambda a, b: jnp.where(core == 0, jnp.concatenate([a, b], 1), jnp.concatenate([b, a], 1))
    grad_out = join(out_mine, last[:64])
    grad_mag = join(mag_mine, last[72:]).reshape(2 * half)
    grad_act = (act_own + act_add.astype(F32)).astype(BF16)
    return (output, grad_act, grad_in, grad_out, grad_mag)


def solution(mesh):
    grid = Mesh(mesh.devices.reshape(8, 4, 8, 2), ("z", "x", "y", "core"))
    every = ("z", "x", "y", "core")
    in_specs = (P(REPLICA, TENSOR), P(TENSOR, None), P(TENSOR, None), P(), P(), P(every, None))
    out_specs = (P(every, None), P(REPLICA, TENSOR), P(TENSOR, None), P(), P())
    return jax.shard_map(program, mesh=grid, in_specs=in_specs, out_specs=out_specs, check_vma=False)
```

```python
import jax
import jax.numpy as jnp
from jax import lax
from jax.experimental import pallas as pl
from jax.experimental.pallas import tpu as pltpu
from jax.sharding import Mesh, PartitionSpec as P


epsilon = 1e-06
F32, BF16 = jnp.float32, jnp.bfloat16
REPLICA = ("z", "x")
TENSOR = ("y", "core")
TILE = 512


def split(value):
    high = value.astype(BF16)
    return high, (value - high.astype(F32)).astype(BF16)


def contract(left, right, dims):
    return lax.dot_general(left, right, ((dims[:1], dims[1:]), ((), ())), preferred_element_type=F32)


def merge_kernel(at_ref, base_ref, wide_ref, pick_ref, out_ref, zt_ref, low_ref, first_ref):
    step = pl.program_id(0)
    ah, al = split(out_ref[...])
    low = contract(wide_ref[...], jnp.concatenate([ah, al, ah, al], 0), (1, 0))
    merged = base_ref[...].astype(F32) + low
    squares = jnp.sum(merged * merged, axis=0, keepdims=True)
    low_ref[...] = merged.astype(BF16)
    ranks = zt_ref[pl.ds(pl.multiple_of(step * 16, 16), 16), :]
    for k in range(4):
        member = 4 * step + k
        for q in range(4):
            first_ref[member, 4 * q : 4 * q + 4, :] = ranks[4 * k : 4 * k + 4, 128 * q : 128 * q + 128]
        for r in range(2):
            first_ref[member, 16 + r : 17 + r, :] = squares[:, 256 * k + 128 * r : 256 * k + 128 * r + 128]
        first_ref[member, 22:24, :] = jnp.zeros((2, 128), F32)

    @pl.when(lax.rem(step, 2) == at_ref[0])
    def _():
        span = pl.ds(pl.multiple_of(at_ref[1] * 128, 128), 128)
        both = contract(pick_ref[...], low_ref[:, span], (1, 0))
        block = both[:32] + both[32:]
        for k in range(8):
            first_ref[2 * k + step // 2, 18:22, :] = block[4 * k : 4 * k + 4]


def merge(at, base, wide, pick, adapter_out, zt):
    rows, cols = base.shape
    tokens = zt.shape[1]
    steps = cols // 1024
    tile = lambda i, c: (0, i)
    whole = lambda i, c: (0, 0)
    return pl.pallas_call(
        merge_kernel,
        out_shape=(jax.ShapeDtypeStruct((rows, cols), BF16), jax.ShapeDtypeStruct((16, 24, 128), F32)),
        grid_spec=pltpu.PrefetchScalarGridSpec(
            num_scalar_prefetch=1,
            grid=(steps,),
            in_specs=[
                pl.BlockSpec((rows, 1024), tile),
                pl.BlockSpec((rows, 256), whole),
                pl.BlockSpec((64, rows), whole),
                pl.BlockSpec((64, 1024), tile),
                pl.BlockSpec((64, tokens), whole),
            ],
            out_specs=(
                pl.BlockSpec((rows, 1024), tile),
                pl.BlockSpec((16, 24, 128), lambda i, c: (0, 0, 0)),
            ),
        ),
        cost_estimate=pl.CostEstimate(flops=1400000000, bytes_accessed=7000000, transcendentals=0),
        name="merge",
    )(at, base, wide, pick, adapter_out, zt)


def forward_kernel(at_ref, a_ref, b_ref, wa_ref, wb_ref, r4_ref, r3_ref, r2_ref, r1_ref, r0_ref, acts):
    @pl.when(pl.program_id(0) == 0)
    def _():
        for k in range(8):
            rows = pl.ds(pl.multiple_of(at_ref[17 + k] * 32, 32), 32)
            acts[32 * k : 32 * k + 32, :256] = a_ref[rows, :]
            acts[32 * k : 32 * k + 32, 256:] = b_ref[rows, :]

    part = contract(acts[...], jnp.concatenate([wa_ref[...], wb_ref[...]], 0), (1, 0))
    r4_ref[...] = part[0:32].astype(BF16)
    r3_ref[...] = part[32:96]
    r2_ref[...] = part[96:160]
    r1_ref[...] = part[160:224]
    r0_ref[...] = part[224:256]


def forward(at, act_own, act_peer, w_own, w_peer):
    tokens, feats = act_own.shape
    cols = w_own.shape[1]
    whole = pl.BlockSpec((tokens, feats), lambda i, c: (0, 0))
    tile = lambda rows: pl.BlockSpec((rows, 1024), lambda i, c: (0, i))
    rows = (32, 64, 64, 64, 32)
    kinds = (BF16, F32, F32, F32, F32)
    return pl.pallas_call(
        forward_kernel,
        out_shape=tuple(jax.ShapeDtypeStruct((r, cols), k) for r, k in zip(rows, kinds)),
        grid_spec=pltpu.PrefetchScalarGridSpec(
            num_scalar_prefetch=1,
            grid=(cols // 1024,),
            in_specs=[whole, whole, tile(feats), tile(feats)],
            out_specs=tuple(tile(r) for r in rows),
            scratch_shapes=[pltpu.VMEM((256, 512), BF16)],
        ),
        cost_estimate=pl.CostEstimate(flops=2 * tokens * feats * cols, bytes_accessed=5000000, transcendentals=0),
        name="forward",
    )(at, act_own, act_peer, w_own, w_peer)


def slope_kernel(
    at_ref, block_ref, hop1_ref, hop2_ref, hop3_ref, hop4_ref, cross_ref, scale_ref, wo_ref, wp_ref, ato_ref, atp_ref,
    scaled_ref, slope_ref, cots,
):
    parts = [block_ref, hop1_ref, hop2_ref, hop3_ref, hop4_ref]
    parts = [(part, r) for part in parts for r in (0, 32)] + [(cross_ref, r) for r in range(0, 192, 32)]
    for k, (part, r) in enumerate(parts):
        cots[pl.ds(pl.multiple_of(at_ref[1 + k] * 32, 32), 32), :] = part[r : r + 32, :]
    cot = cots[...]
    slope = jnp.sum(contract(ato_ref[...], cot, (1, 0)) * wo_ref[...].astype(F32), axis=0, keepdims=True)
    slope = slope + jnp.sum(contract(atp_ref[...], cot, (1, 0)) * wp_ref[...].astype(F32), axis=0, keepdims=True)
    scaled_ref[...] = (cot.astype(F32) * scale_ref[...]).astype(BF16)
    for q in range(8):
        row = slope[:, 128 * q : 128 * q + 128]
        for k in range(8):
            slope_ref[k, q : q + 1, :] = row


def slopes(at, block, hops, hop4, crossed, scale, w_own, w_peer, at_own, at_peer):
    cols = hop4.shape[1]
    feats, tokens = at_own.shape
    steps = cols // 1024
    whole = lambda i, c: (0, 0)
    tile = lambda i, c: (0, i)
    side = lambda i, c: (0, c[0] * steps + i)
    return pl.pallas_call(
        slope_kernel,
        out_shape=(jax.ShapeDtypeStruct((tokens, cols), BF16), jax.ShapeDtypeStruct((8, 16, 128), F32)),
        grid_spec=pltpu.PrefetchScalarGridSpec(
            num_scalar_prefetch=1,
            grid=(steps,),
            in_specs=[pl.BlockSpec((64, 1024), side)] * 4
            + [
                pl.BlockSpec((64, 1024), tile),
                pl.BlockSpec((192, 1024), tile),
                pl.BlockSpec((1, 1024), side),
                pl.BlockSpec((feats, 1024), side),
                pl.BlockSpec((feats, 1024), side),
                pl.BlockSpec((feats, tokens), whole),
                pl.BlockSpec((feats, tokens), whole),
            ],
            out_specs=(pl.BlockSpec((tokens, 1024), tile), pl.BlockSpec((8, 8, 128), lambda i, c: (0, i, 0))),
            scratch_shapes=[pltpu.VMEM((tokens, 1024), BF16)],
        ),
        cost_estimate=pl.CostEstimate(flops=2200000000, bytes_accessed=8000000, transcendentals=0),
        name="slopes",
    )(at, block, *hops, hop4, crossed, scale, w_own, w_peer, at_own, at_peer)


def backward_kernel(
    at_ref, scaled_ref, wo_ref, wp_ref, ato_ref, atp_ref, second_ref, out_ref,
    gao_ref, gap_ref, low_ref, sum_own, sum_peer, sum_y, zt,
):
    step = pl.program_id(0)

    @pl.when(step == 0)
    def _():
        for m in range(16):
            for q in range(4):
                zt[4 * m : 4 * m + 4, 128 * q : 128 * q + 128] = second_ref[m, 4 * q : 4 * q + 4, :]

    scaled = scaled_ref[...]
    both = contract(jnp.concatenate(split(zt[...]), 0), scaled, (1, 0))
    p = (both[:64] + both[64:]).astype(BF16)
    for q in range(4):
        for r in range(2):
            low_ref[8 * step + 2 * q + r, 0:32, :] = p[32 * r : 32 * r + 32, 128 * q : 128 * q + 128]
    own = contract(scaled, wo_ref[...], (1, 1))
    peer = contract(scaled, wp_ref[...], (1, 1))
    y = contract(scaled, jnp.concatenate(split(out_ref[...]), 0), (1, 1))

    @pl.when(step == 0)
    def _():
        sum_own[...] = own
        sum_peer[...] = peer
        sum_y[...] = y

    @pl.when(step > 0)
    def _():
        sum_own[...] += own
        sum_peer[...] += peer
        sum_y[...] += y

    @pl.when(step == pl.num_programs(0) - 1)
    def _():
        gao_ref[...] = sum_own[...]
        gap_ref[...] = sum_peer[...].astype(BF16)
        pair = jnp.concatenate(split(sum_y[...]), 0)
        for k, ref in enumerate((ato_ref, atp_ref)):
            both = contract(jnp.concatenate([ref[...], ref[...]], 1), pair, (1, 0)).T
            both = (both[:64] + both[64:]).astype(BF16)
            for a in range(8):
                for q in range(2):
                    low_ref[4 * a + 2 * k + q, 32:40, :] = both[8 * a : 8 * a + 8, 128 * q : 128 * q + 128]


def backward(at, scaled, w_own, w_peer, at_own, at_peer, second, adapter_out):
    tokens, cols = scaled.shape
    feats = at_own.shape[0]
    steps = cols // TILE
    whole = lambda i, c: (0, 0)
    tile = lambda i, c: (0, i)
    side = lambda i, c: (0, c[0] * steps + i)
    return pl.pallas_call(
        backward_kernel,
        out_shape=(
            jax.ShapeDtypeStruct((tokens, feats), F32),
            jax.ShapeDtypeStruct((tokens, feats), BF16),
            jax.ShapeDtypeStruct((32, 40, 128), BF16),
        ),
        grid_spec=pltpu.PrefetchScalarGridSpec(
            num_scalar_prefetch=1,
            grid=(steps,),
            in_specs=[
                pl.BlockSpec((tokens, TILE), tile),
                pl.BlockSpec((feats, TILE), side),
                pl.BlockSpec((feats, TILE), side),
                pl.BlockSpec((feats, tokens), whole),
                pl.BlockSpec((feats, tokens), whole),
                pl.BlockSpec((16, 24, 128), lambda i, c: (0, 0, 0)),
                pl.BlockSpec((64, TILE), side),
            ],
            out_specs=(
                pl.BlockSpec((tokens, feats), whole),
                pl.BlockSpec((tokens, feats), whole),
                pl.BlockSpec((32, 40, 128), lambda i, c: (0, 0, 0)),
            ),
            scratch_shapes=[
                pltpu.VMEM((tokens, feats), F32),
                pltpu.VMEM((tokens, feats), F32),
                pltpu.VMEM((tokens, 128), F32),
                pltpu.VMEM((64, tokens), F32),
            ],
        ),
        cost_estimate=pl.CostEstimate(flops=3000000000, bytes_accessed=6000000, transcendentals=0),
        name="backward",
    )(at, scaled, w_own, w_peer, at_own, at_peer, second, adapter_out)


def combine_kernel(at_ref, got_ref, second_ref, norm_ref, size_ref, o_ref):
    total = jnp.sum(got_ref[...].astype(F32), axis=0)
    norm = norm_ref[...]
    mag = (total[40:41] + total[41:42]) / norm
    coeff = -mag * size_ref[...] / (norm * norm)
    q = jnp.concatenate([second_ref[2 * k + at_ref[0], 18:22, :] for k in range(8)], 0)
    high, low = split(mag)
    out = (total[0:32] + q * coeff).astype(BF16)
    o_ref[...] = jnp.broadcast_to(jnp.concatenate([out, total[32:40].astype(BF16), high, low], 0), o_ref.shape)


def combine(at, got, second, norm, size):
    column = pl.BlockSpec((1, 128), lambda i, c: (0, c[0] * 16 + c[1]))
    block = pl.BlockSpec(got.shape, lambda i, c: (0, 0, 0))
    return pl.pallas_call(
        combine_kernel,
        out_shape=jax.ShapeDtypeStruct(got.shape, BF16),
        grid_spec=pltpu.PrefetchScalarGridSpec(
            num_scalar_prefetch=1,
            grid=(1,),
            in_specs=[block, pl.BlockSpec((16, 24, 128), lambda i, c: (0, 0, 0)), column, column],
            out_specs=block,
        ),
        cost_estimate=pl.CostEstimate(flops=2000000, bytes_accessed=700000, transcendentals=0),
        name="combine",
    )(at, got, second, norm, size)


def finish_kernel(at_ref, got_ref, wo_ref, wp_ref, a_ref, norm_ref, size_ref, last_ref, own_ref, sum_own, sum_peer):
    step = pl.program_id(0)
    mags = []
    for q in range(8):
        j = 16 * step + 2 * q
        mags.append(got_ref[j, 40:41, :].astype(F32) + got_ref[j, 41:42, :].astype(F32))
        span = pl.ds(pl.multiple_of(step * 1024 + 128 * q, 128), 128)
        for r in range(2):
            last_ref[32 * r : 32 * r + 32, span] = got_ref[j + r, 0:32, :].astype(F32)
    mag = jnp.concatenate(mags, 1)
    last_ref[64:72, pl.ds(pl.multiple_of(step * 1024, 1024), 1024)] = jnp.broadcast_to(mag, (8, 1024))
    norm = norm_ref[...]
    coeff = -mag * size_ref[...] / (norm * norm)
    pair = jnp.concatenate(split(a_ref[...] * coeff), 0)
    own = contract(wo_ref[...], pair, (1, 1))
    peer = contract(wp_ref[...], pair, (1, 1))

    @pl.when(step == 0)
    def _():
        sum_own[...] = own
        sum_peer[...] = peer

    @pl.when(step > 0)
    def _():
        own_total, peer_total = (sum_own[...] + own).T, (sum_peer[...] + peer).T
        own_ref[...] = own_total[:64] + own_total[64:]
        last_ref[0:64, 2048:2304] = peer_total[:64] + peer_total[64:]
        last_ref[64:72, 2048:2304] = jnp.zeros((8, 256), F32)
        for a in range(8):
            rows = slice(8 * a, 8 * a + 8)
            for q in range(2):
                span = slice(128 * q, 128 * q + 128)
                own_ref[rows, span] += got_ref[4 * a + q, 32:40, :].astype(F32)
                last_ref[rows, 2048 + 128 * q : 2176 + 128 * q] += got_ref[4 * a + 2 + q, 32:40, :].astype(F32)


def finish(at, got, w_own, w_peer, adapter_out, norm, size):
    side = lambda i, c: (0, c[0] * 2 + i)
    whole = lambda i, c: (0, 0)
    return pl.pallas_call(
        finish_kernel,
        out_shape=(jax.ShapeDtypeStruct((72, 2304), F32), jax.ShapeDtypeStruct((64, 256), F32)),
        grid_spec=pltpu.PrefetchScalarGridSpec(
            num_scalar_prefetch=1,
            grid=(2,),
            in_specs=[
                pl.BlockSpec(got.shape, lambda i, c: (0, 0, 0)),
                pl.BlockSpec((256, 1024), side),
                pl.BlockSpec((256, 1024), side),
                pl.BlockSpec((64, 1024), side),
                pl.BlockSpec((1, 1024), side),
                pl.BlockSpec((1, 1024), side),
            ],
            out_specs=(pl.BlockSpec((72, 2304), whole), pl.BlockSpec((64, 256), whole)),
            scratch_shapes=[pltpu.VMEM((256, 128), F32), pltpu.VMEM((256, 128), F32)],
        ),
        cost_estimate=pl.CostEstimate(flops=600000000, bytes_accessed=3000000, transcendentals=0),
        name="finish",
    )(at, got, w_own, w_peer, adapter_out, norm, size)


def program(activations, base_weight, adapter_in, adapter_out, magnitude, cotangent):
    core = lax.axis_index("core")
    y = lax.axis_index("y")
    replica = lax.axis_index(REPLICA)
    sides = lax.axis_size("y")
    replicas = lax.axis_size(REPLICA)
    half = adapter_out.shape[1] // 2
    hops = [(2 * s, 2 * ((s + 1) % sides)) for s in range(sides)]
    hops += [(2 * s + 1, 2 * ((s - 1) % sides) + 1) for s in range(sides)]

    def swap(value):
        return lax.ppermute(value, "core", [(0, 1), (1, 0)])

    def shift(value):
        return lax.ppermute(value, TENSOR, hops)

    def exchange(value, axes):
        return lax.all_to_all(value, axes, 0, 0)

    def spread(value, axes):
        return exchange(jnp.broadcast_to(value, (lax.axis_size(axes),) + value.shape), axes)

    mine = lambda value: lax.dynamic_slice_in_dim(value, core * half, half, 1)
    other = lambda value: lax.dynamic_slice_in_dim(value, (1 - core) * half, half, 1)

    block = jnp.concatenate([cotangent, swap(cotangent)], 0)
    hop1 = shift(block)
    hop2 = shift(hop1)
    hop3 = shift(hop2)
    sign = 1 - 2 * core
    near, far = [], []
    for k in range(5):
        chip = lax.rem(y - sign * k + sides, sides) * 2
        near += [chip + core, chip + 1 - core]
    for k in range(1, 4):
        chip = lax.rem(y + sign * k + sides, sides) * 2
        far += [chip + 1 - core, chip + core]
    rows = [lax.rem(y + sign * 4 + sides, sides) * 2 + core]
    for k in (3, 2, 1):
        chip = lax.rem(y + sign * k + sides, sides) * 2
        rows += [chip + core, chip + 1 - core]
    rows += [2 * y + core]
    at = jnp.stack([core] + near + far + rows).astype(jnp.int32)

    act_peer = swap(activations)
    high = lax.reduce_precision(adapter_in, 8, 7)
    rest = (adapter_in - high).astype(BF16)
    high = high.astype(BF16)
    wide = jnp.concatenate([high, high, rest, rest], 1)
    pair = jnp.concatenate([high.T, rest.T], 0)
    window, part = replica // 2, lax.rem(replica, 2)
    pick = jnp.concatenate([lax.dynamic_slice_in_dim(pair, 64 * k + part * 32, 32, 0) for k in range(2)], 0)
    at_own = activations.T
    z = contract(pair, at_own, (1, 0))
    place = jnp.stack([window // 8, lax.rem(window, 8)]).astype(jnp.int32)
    w_own, first = merge(place, base_weight, wide, pick, adapter_out, z[:64] + z[64:])
    w_peer = swap(w_own)
    first = jnp.sum(exchange(first, TENSOR), axis=0)
    second = spread(first, TENSOR)
    hop4 = shift(mine(hop3))
    crossed = swap(jnp.concatenate([other(hop1), other(hop2), other(hop3)], 0))

    square_sum = second[:, 16:18].reshape(1, 2 * half)
    col_norm = jnp.sqrt(square_sum + epsilon)
    magnitude = magnitude.reshape(1, 2 * half)
    col_scale = magnitude / col_norm
    r4, r3, r2, r1, r0 = forward(at, activations, act_peer, w_own, w_peer)
    got = shift(r4).astype(F32)
    got = shift(jnp.concatenate([r3[:32] + got, r3[32:]], 0).astype(BF16)).astype(F32)
    got = shift((r2 + got).astype(BF16)).astype(F32)
    got = shift((r1 + got).astype(BF16))
    summed = r0 + got[:32].astype(F32) + swap(got[32:]).astype(F32)
    output = (summed * col_scale).astype(BF16)

    at_peer = act_peer.T
    scaled, slope = slopes(at, block, (hop1, hop2, hop3), hop4, crossed, col_scale, w_own, w_peer, at_own, at_peer)
    slope = jnp.sum(exchange(slope, "y"), axis=0)
    high = lax.reduce_precision(slope, 8, 7)
    slope = jnp.stack([high, slope - high], 1).astype(BF16)
    slope = jnp.broadcast_to(slope[:, None], (16, 2, 2, 128)).reshape(replicas, 2, 128)
    act_own, act_send, low = backward(at, scaled, w_own, w_peer, at_own, at_peer, second, adapter_out)
    low = exchange(jnp.concatenate([low, slope], 1), REPLICA)
    place = jnp.stack([core, window]).astype(jnp.int32)
    low = exchange(combine(place, low, second, col_norm, magnitude), REPLICA)
    act_add = swap(act_send)
    payload, in_own = finish(at, low, w_own, w_peer, adapter_out, col_norm, magnitude)
    last = swap(payload)
    grad_in = (in_own + last[:64, half:]).T
    join = lambda a, b: jnp.where(core == 0, jnp.concatenate([a, b], 1), jnp.concatenate([b, a], 1))
    grad_out = join(payload[:64, :half], last[:64, :half])
    grad_mag = join(payload[64:65, :half], last[64:65, :half]).reshape(2 * half)
    grad_act = (act_own + act_add.astype(F32)).astype(BF16)
    return (output, grad_act, grad_in, grad_out, grad_mag)


def solution(mesh):
    grid = Mesh(mesh.devices.reshape(8, 4, 8, 2), ("z", "x", "y", "core"))
    every = ("z", "x", "y", "core")
    in_specs = (P(REPLICA, TENSOR), P(TENSOR, None), P(TENSOR, None), P(), P(), P(every, None))
    out_specs = (P(every, None), P(REPLICA, TENSOR), P(TENSOR, None), P(), P())
    return jax.shard_map(program, mesh=grid, in_specs=in_specs, out_specs=out_specs, check_vma=False)
```

```python
import jax
import jax.numpy as jnp
from jax import lax
from jax.experimental import pallas as pl
from jax.experimental.pallas import tpu as pltpu
from jax.sharding import Mesh, PartitionSpec as P


epsilon = 1e-06
F32, BF16 = jnp.float32, jnp.bfloat16
REPLICA = ("z", "x")
TENSOR = ("y", "core")
TILE = 512


def split(value):
    high = value.astype(BF16)
    return high, (value - high.astype(F32)).astype(BF16)


def contract(left, right, dims):
    return lax.dot_general(left, right, ((dims[:1], dims[1:]), ((), ())), preferred_element_type=F32)


def merge_kernel(at_ref, base_ref, wide_ref, pair_ref, out_ref, z_ref, low_ref, first_ref):
    step = pl.program_id(0)
    ah, al = split(out_ref[...])
    low = contract(wide_ref[...], jnp.concatenate([ah, al, ah, al], 0), (1, 0))
    merged = base_ref[...].astype(F32) + low
    squares = jnp.sum(merged * merged, axis=0, keepdims=True)
    low_ref[...] = merged.astype(BF16)
    ranks = z_ref[pl.ds(pl.multiple_of(step * 16, 16), 16), :] + z_ref[pl.ds(pl.multiple_of(64 + step * 16, 16), 16), :]
    for k in range(4):
        member = 4 * step + k
        for q in range(4):
            first_ref[member, 4 * q : 4 * q + 4, :] = ranks[4 * k : 4 * k + 4, 128 * q : 128 * q + 128]
        for r in range(2):
            first_ref[member, 16 + r : 17 + r, :] = squares[:, 256 * k + 128 * r : 256 * k + 128 * r + 128]
        first_ref[member, 22:24, :] = jnp.zeros((2, 128), F32)

    @pl.when(lax.rem(step, 2) == at_ref[25])
    def _():
        span = pl.ds(pl.multiple_of(at_ref[26] * 128, 128), 128)
        rows = [pair_ref[pl.ds(pl.multiple_of(64 * k + at_ref[28] * 32, 32), 32), :] for k in range(2)]
        both = contract(jnp.concatenate(rows, 0), low_ref[:, span], (1, 0))
        block = both[:32] + both[32:]
        for k in range(8):
            first_ref[2 * k + step // 2, 18:22, :] = block[4 * k : 4 * k + 4]


def merge(at, base, wide, pair, adapter_out, z):
    rows, cols = base.shape
    tokens = z.shape[1]
    steps = cols // 1024
    tile = lambda i, c: (0, i)
    whole = lambda i, c: (0, 0)
    return pl.pallas_call(
        merge_kernel,
        out_shape=(jax.ShapeDtypeStruct((rows, cols), BF16), jax.ShapeDtypeStruct((16, 24, 128), F32)),
        grid_spec=pltpu.PrefetchScalarGridSpec(
            num_scalar_prefetch=1,
            grid=(steps,),
            in_specs=[
                pl.BlockSpec((rows, 1024), tile),
                pl.BlockSpec((rows, 256), whole),
                pl.BlockSpec((128, rows), whole),
                pl.BlockSpec((64, 1024), tile),
                pl.BlockSpec((128, tokens), whole),
            ],
            out_specs=(
                pl.BlockSpec((rows, 1024), tile),
                pl.BlockSpec((16, 24, 128), lambda i, c: (0, 0, 0)),
            ),
        ),
        cost_estimate=pl.CostEstimate(flops=1400000000, bytes_accessed=7000000, transcendentals=0),
        name="merge",
    )(at, base, wide, pair, adapter_out, z)


def forward_kernel(at_ref, a_ref, b_ref, wa_ref, wb_ref, r4_ref, r3_ref, r2_ref, r1_ref, r0_ref, acts):
    @pl.when(pl.program_id(0) == 0)
    def _():
        for k in range(8):
            rows = pl.ds(pl.multiple_of(at_ref[17 + k] * 32, 32), 32)
            acts[32 * k : 32 * k + 32, :256] = a_ref[rows, :]
            acts[32 * k : 32 * k + 32, 256:] = b_ref[rows, :]

    part = contract(acts[...], jnp.concatenate([wa_ref[...], wb_ref[...]], 0), (1, 0))
    r4_ref[...] = part[0:32].astype(BF16)
    r3_ref[...] = part[32:96]
    r2_ref[...] = part[96:160]
    r1_ref[...] = part[160:224]
    r0_ref[...] = part[224:256]


def forward(at, act_own, act_peer, w_own, w_peer):
    tokens, feats = act_own.shape
    cols = w_own.shape[1]
    whole = pl.BlockSpec((tokens, feats), lambda i, c: (0, 0))
    tile = lambda rows: pl.BlockSpec((rows, 1024), lambda i, c: (0, i))
    rows = (32, 64, 64, 64, 32)
    kinds = (BF16, F32, F32, F32, F32)
    return pl.pallas_call(
        forward_kernel,
        out_shape=tuple(jax.ShapeDtypeStruct((r, cols), k) for r, k in zip(rows, kinds)),
        grid_spec=pltpu.PrefetchScalarGridSpec(
            num_scalar_prefetch=1,
            grid=(cols // 1024,),
            in_specs=[whole, whole, tile(feats), tile(feats)],
            out_specs=tuple(tile(r) for r in rows),
            scratch_shapes=[pltpu.VMEM((256, 512), BF16)],
        ),
        cost_estimate=pl.CostEstimate(flops=2 * tokens * feats * cols, bytes_accessed=5000000, transcendentals=0),
        name="forward",
    )(at, act_own, act_peer, w_own, w_peer)


def slope_kernel(
    at_ref, block_ref, hop1_ref, hop2_ref, hop3_ref, hop4_ref, cross_ref, scale_ref, wo_ref, wp_ref, ato_ref, atp_ref,
    scaled_ref, slope_ref, cots,
):
    parts = [block_ref, hop1_ref, hop2_ref, hop3_ref, hop4_ref]
    parts = [(part, r) for part in parts for r in (0, 32)] + [(cross_ref, r) for r in range(0, 192, 32)]
    for k, (part, r) in enumerate(parts):
        cots[pl.ds(pl.multiple_of(at_ref[1 + k] * 32, 32), 32), :] = part[r : r + 32, :]
    cot = cots[...]
    slope = jnp.sum(contract(ato_ref[...], cot, (1, 0)) * wo_ref[...].astype(F32), axis=0, keepdims=True)
    slope = slope + jnp.sum(contract(atp_ref[...], cot, (1, 0)) * wp_ref[...].astype(F32), axis=0, keepdims=True)
    scaled_ref[...] = (cot.astype(F32) * scale_ref[...]).astype(BF16)
    for q in range(8):
        row = slope[:, 128 * q : 128 * q + 128]
        for k in range(8):
            slope_ref[k, q : q + 1, :] = row


def slopes(at, block, hops, hop4, crossed, scale, w_own, w_peer, at_own, at_peer):
    cols = hop4.shape[1]
    feats, tokens = at_own.shape
    steps = cols // 1024
    whole = lambda i, c: (0, 0)
    tile = lambda i, c: (0, i)
    side = lambda i, c: (0, c[0] * steps + i)
    return pl.pallas_call(
        slope_kernel,
        out_shape=(jax.ShapeDtypeStruct((tokens, cols), BF16), jax.ShapeDtypeStruct((8, 16, 128), F32)),
        grid_spec=pltpu.PrefetchScalarGridSpec(
            num_scalar_prefetch=1,
            grid=(steps,),
            in_specs=[pl.BlockSpec((64, 1024), side)] * 4
            + [
                pl.BlockSpec((64, 1024), tile),
                pl.BlockSpec((192, 1024), tile),
                pl.BlockSpec((1, 1024), side),
                pl.BlockSpec((feats, 1024), side),
                pl.BlockSpec((feats, 1024), side),
                pl.BlockSpec((feats, tokens), whole),
                pl.BlockSpec((feats, tokens), whole),
            ],
            out_specs=(pl.BlockSpec((tokens, 1024), tile), pl.BlockSpec((8, 8, 128), lambda i, c: (0, i, 0))),
            scratch_shapes=[pltpu.VMEM((tokens, 1024), BF16)],
        ),
        cost_estimate=pl.CostEstimate(flops=2200000000, bytes_accessed=8000000, transcendentals=0),
        name="slopes",
    )(at, block, *hops, hop4, crossed, scale, w_own, w_peer, at_own, at_peer)


def backward_kernel(
    at_ref, scaled_ref, wo_ref, wp_ref, ato_ref, atp_ref, second_ref, out_ref,
    gao_ref, gap_ref, low_ref, sum_own, sum_peer, sum_y, zt,
):
    step = pl.program_id(0)

    @pl.when(step == 0)
    def _():
        for m in range(16):
            for q in range(4):
                zt[4 * m : 4 * m + 4, 128 * q : 128 * q + 128] = second_ref[m, 4 * q : 4 * q + 4, :]

    scaled = scaled_ref[...]
    both = contract(jnp.concatenate(split(zt[...]), 0), scaled, (1, 0))
    p = (both[:64] + both[64:]).astype(BF16)
    for q in range(4):
        for r in range(2):
            low_ref[8 * step + 2 * q + r, 0:32, :] = p[32 * r : 32 * r + 32, 128 * q : 128 * q + 128]
    own = contract(scaled, wo_ref[...], (1, 1))
    peer = contract(scaled, wp_ref[...], (1, 1))
    y = contract(scaled, jnp.concatenate(split(out_ref[...]), 0), (1, 1))

    @pl.when(step == 0)
    def _():
        sum_own[...] = own
        sum_peer[...] = peer
        sum_y[...] = y

    @pl.when(step > 0)
    def _():
        sum_own[...] += own
        sum_peer[...] += peer
        sum_y[...] += y

    @pl.when(step == pl.num_programs(0) - 1)
    def _():
        gao_ref[...] = sum_own[...]
        gap_ref[...] = sum_peer[...].astype(BF16)
        low_ref[:, 40:48, :] = jnp.zeros((32, 8, 128), BF16)
        pair = jnp.concatenate(split(sum_y[...]), 0)
        for k, ref in enumerate((ato_ref, atp_ref)):
            both = contract(jnp.concatenate([ref[...], ref[...]], 1), pair, (1, 0)).T
            both = (both[:64] + both[64:]).astype(BF16)
            for a in range(8):
                for q in range(2):
                    low_ref[4 * a + 2 * k + q, 32:40, :] = both[8 * a : 8 * a + 8, 128 * q : 128 * q + 128]


def backward(at, scaled, w_own, w_peer, at_own, at_peer, second, adapter_out):
    tokens, cols = scaled.shape
    feats = at_own.shape[0]
    steps = cols // TILE
    whole = lambda i, c: (0, 0)
    tile = lambda i, c: (0, i)
    side = lambda i, c: (0, c[0] * steps + i)
    return pl.pallas_call(
        backward_kernel,
        out_shape=(
            jax.ShapeDtypeStruct((tokens, feats), F32),
            jax.ShapeDtypeStruct((tokens, feats), BF16),
            jax.ShapeDtypeStruct((32, 48, 128), BF16),
        ),
        grid_spec=pltpu.PrefetchScalarGridSpec(
            num_scalar_prefetch=1,
            grid=(steps,),
            in_specs=[
                pl.BlockSpec((tokens, TILE), tile),
                pl.BlockSpec((feats, TILE), side),
                pl.BlockSpec((feats, TILE), side),
                pl.BlockSpec((feats, tokens), whole),
                pl.BlockSpec((feats, tokens), whole),
                pl.BlockSpec((16, 24, 128), lambda i, c: (0, 0, 0)),
                pl.BlockSpec((64, TILE), side),
            ],
            out_specs=(
                pl.BlockSpec((tokens, feats), whole),
                pl.BlockSpec((tokens, feats), whole),
                pl.BlockSpec((32, 48, 128), lambda i, c: (0, 0, 0)),
            ),
            scratch_shapes=[
                pltpu.VMEM((tokens, feats), F32),
                pltpu.VMEM((tokens, feats), F32),
                pltpu.VMEM((tokens, 128), F32),
                pltpu.VMEM((64, tokens), F32),
            ],
        ),
        cost_estimate=pl.CostEstimate(flops=3000000000, bytes_accessed=6000000, transcendentals=0),
        name="backward",
    )(at, scaled, w_own, w_peer, at_own, at_peer, second, adapter_out)


def pack_kernel(got_ref, low_ref, o_ref):
    slope = jnp.sum(got_ref[...], axis=0)
    high, low = split(slope)
    high, low = high.astype(F32), low.astype(F32)
    none = jnp.zeros((6, 128), F32)
    for k in range(16):
        rows = jnp.concatenate([high[k : k + 1], low[k : k + 1], none], 0).astype(BF16)
        o_ref[2 * k] = rows
        o_ref[2 * k + 1] = rows


def pack(got, low):
    return pl.pallas_call(
        pack_kernel,
        out_shape=jax.ShapeDtypeStruct(low.shape, BF16),
        grid=(1,),
        in_specs=[pl.BlockSpec(got.shape, lambda i: (0, 0, 0)), pl.BlockSpec(memory_space=pl.ANY)],
        out_specs=pl.BlockSpec((32, 8, 128), lambda i: (0, 5, 0)),
        input_output_aliases={1: 0},
        cost_estimate=pl.CostEstimate(flops=20000, bytes_accessed=130000, transcendentals=0),
        name="pack",
    )(got, low)


def combine_kernel(at_ref, got_ref, second_ref, norm_ref, size_ref, o_ref):
    total = jnp.sum(got_ref[...].astype(F32), axis=0)
    norm = norm_ref[...]
    mag = (total[40:41] + total[41:42]) / norm
    coeff = -mag * size_ref[...] / (norm * norm)
    q = jnp.concatenate([second_ref[2 * k + at_ref[0], 18:22, :] for k in range(8)], 0)
    high, low = split(mag)
    out = (total[0:32] + q * coeff).astype(BF16)
    o_ref[...] = jnp.broadcast_to(jnp.concatenate([out, total[32:40].astype(BF16), high, low, jnp.zeros((6, 128), BF16)], 0), o_ref.shape)


def combine(at, got, second, norm, size):
    column = pl.BlockSpec((1, 128), lambda i, c: (0, c[0] * 16 + c[27]))
    block = pl.BlockSpec(got.shape, lambda i, c: (0, 0, 0))
    return pl.pallas_call(
        combine_kernel,
        out_shape=jax.ShapeDtypeStruct(got.shape, BF16),
        grid_spec=pltpu.PrefetchScalarGridSpec(
            num_scalar_prefetch=1,
            grid=(1,),
            in_specs=[block, pl.BlockSpec((16, 24, 128), lambda i, c: (0, 0, 0)), column, column],
            out_specs=block,
        ),
        cost_estimate=pl.CostEstimate(flops=2000000, bytes_accessed=700000, transcendentals=0),
        name="combine",
    )(at, got, second, norm, size)


def finish_kernel(at_ref, got_ref, wo_ref, wp_ref, a_ref, norm_ref, size_ref, last_ref, own_ref, sum_own, sum_peer):
    step = pl.program_id(0)
    mags = []
    for q in range(8):
        j = 16 * step + 2 * q
        mags.append(got_ref[j, 40:41, :].astype(F32) + got_ref[j, 41:42, :].astype(F32))
        span = pl.ds(pl.multiple_of(step * 1024 + 128 * q, 128), 128)
        for r in range(2):
            last_ref[32 * r : 32 * r + 32, span] = got_ref[j + r, 0:32, :].astype(F32)
    mag = jnp.concatenate(mags, 1)
    last_ref[64:72, pl.ds(pl.multiple_of(step * 1024, 1024), 1024)] = jnp.broadcast_to(mag, (8, 1024))
    norm = norm_ref[...]
    coeff = -mag * size_ref[...] / (norm * norm)
    pair = jnp.concatenate(split(a_ref[...] * coeff), 0)
    own = contract(wo_ref[...], pair, (1, 1))
    peer = contract(wp_ref[...], pair, (1, 1))

    @pl.when(step == 0)
    def _():
        sum_own[...] = own
        sum_peer[...] = peer

    @pl.when(step > 0)
    def _():
        own_total, peer_total = (sum_own[...] + own).T, (sum_peer[...] + peer).T
        own_ref[...] = own_total[:64] + own_total[64:]
        last_ref[0:64, 2048:2304] = peer_total[:64] + peer_total[64:]
        last_ref[64:72, 2048:2304] = jnp.zeros((8, 256), F32)
        for a in range(8):
            rows = slice(8 * a, 8 * a + 8)
            for q in range(2):
                span = slice(128 * q, 128 * q + 128)
                own_ref[rows, span] += got_ref[4 * a + q, 32:40, :].astype(F32)
                last_ref[rows, 2048 + 128 * q : 2176 + 128 * q] += got_ref[4 * a + 2 + q, 32:40, :].astype(F32)


def finish(at, got, w_own, w_peer, adapter_out, norm, size):
    side = lambda i, c: (0, c[0] * 2 + i)
    whole = lambda i, c: (0, 0)
    return pl.pallas_call(
        finish_kernel,
        out_shape=(jax.ShapeDtypeStruct((72, 2304), F32), jax.ShapeDtypeStruct((64, 256), F32)),
        grid_spec=pltpu.PrefetchScalarGridSpec(
            num_scalar_prefetch=1,
            grid=(2,),
            in_specs=[
                pl.BlockSpec(got.shape, lambda i, c: (0, 0, 0)),
                pl.BlockSpec((256, 1024), side),
                pl.BlockSpec((256, 1024), side),
                pl.BlockSpec((64, 1024), side),
                pl.BlockSpec((1, 1024), side),
                pl.BlockSpec((1, 1024), side),
            ],
            out_specs=(pl.BlockSpec((72, 2304), whole), pl.BlockSpec((64, 256), whole)),
            scratch_shapes=[pltpu.VMEM((256, 128), F32), pltpu.VMEM((256, 128), F32)],
        ),
        cost_estimate=pl.CostEstimate(flops=600000000, bytes_accessed=3000000, transcendentals=0),
        name="finish",
    )(at, got, w_own, w_peer, adapter_out, norm, size)


def join_kernel(at_ref, mine_ref, other_ref, out_ref, mag_ref):
    cols = out_ref.shape[1] // 2
    for ref, side in ((mine_ref, at_ref[0]), (other_ref, 1 - at_ref[0])):
        span = pl.ds(pl.multiple_of(side * cols, cols), cols)
        out_ref[:, span] = ref[0:64, 0:cols]
        mag_ref[:, span] = ref[64:72, 0:cols]


def join(at, mine, other):
    block = pl.BlockSpec(mine.shape, lambda i, c: (0, 0))
    return pl.pallas_call(
        join_kernel,
        out_shape=(jax.ShapeDtypeStruct((64, 4096), F32), jax.ShapeDtypeStruct((8, 4096), F32)),
        grid_spec=pltpu.PrefetchScalarGridSpec(
            num_scalar_prefetch=1,
            grid=(1,),
            in_specs=[block, block],
            out_specs=(pl.BlockSpec((64, 4096), lambda i, c: (0, 0)), pl.BlockSpec((8, 4096), lambda i, c: (0, 0))),
        ),
        cost_estimate=pl.CostEstimate(flops=100000, bytes_accessed=2500000, transcendentals=0),
        name="join",
    )(at, mine, other)


def program(activations, base_weight, adapter_in, adapter_out, magnitude, cotangent):
    core = lax.axis_index("core")
    y = lax.axis_index("y")
    replica = lax.axis_index(REPLICA)
    sides = lax.axis_size("y")
    half = adapter_out.shape[1] // 2
    hops = [(2 * s, 2 * ((s + 1) % sides)) for s in range(sides)]
    hops += [(2 * s + 1, 2 * ((s - 1) % sides) + 1) for s in range(sides)]

    def swap(value):
        return lax.ppermute(value, "core", [(0, 1), (1, 0)])

    def shift(value):
        return lax.ppermute(value, TENSOR, hops)

    def exchange(value, axes):
        return lax.all_to_all(value, axes, 0, 0)

    def spread(value, axes):
        return exchange(jnp.broadcast_to(value, (lax.axis_size(axes),) + value.shape), axes)

    mine = lambda value: lax.dynamic_slice_in_dim(value, core * half, half, 1)
    other = lambda value: lax.dynamic_slice_in_dim(value, (1 - core) * half, half, 1)

    block = jnp.concatenate([cotangent, swap(cotangent)], 0)
    hop1 = shift(block)
    hop2 = shift(hop1)
    hop3 = shift(hop2)
    sign = 1 - 2 * core
    near, far = [], []
    for k in range(5):
        chip = lax.rem(y - sign * k + sides, sides) * 2
        near += [chip + core, chip + 1 - core]
    for k in range(1, 4):
        chip = lax.rem(y + sign * k + sides, sides) * 2
        far += [chip + 1 - core, chip + core]
    rows = [lax.rem(y + sign * 4 + sides, sides) * 2 + core]
    for k in (3, 2, 1):
        chip = lax.rem(y + sign * k + sides, sides) * 2
        rows += [chip + core, chip + 1 - core]
    rows += [2 * y + core]
    window, part = replica // 2, lax.rem(replica, 2)
    at = [core] + near + far + rows + [window // 8, lax.rem(window, 8), window, part]
    at = jnp.stack(at).astype(jnp.int32)

    act_peer = swap(activations)
    high = lax.reduce_precision(adapter_in, 8, 7)
    rest = (adapter_in - high).astype(BF16)
    high = high.astype(BF16)
    wide = jnp.concatenate([high, high, rest, rest], 1)
    pair = jnp.concatenate([high.T, rest.T], 0)
    at_own = activations.T
    z = contract(pair, at_own, (1, 0))
    w_own, first = merge(at, base_weight, wide, pair, adapter_out, z)
    w_peer = swap(w_own)
    first = jnp.sum(exchange(first, TENSOR), axis=0)
    second = spread(first, TENSOR)
    hop4 = shift(mine(hop3))
    crossed = swap(jnp.concatenate([other(hop1), other(hop2), other(hop3)], 0))

    square_sum = second[:, 16:18].reshape(1, 2 * half)
    col_norm = jnp.sqrt(square_sum + epsilon)
    magnitude = magnitude.reshape(1, 2 * half)
    col_scale = magnitude / col_norm
    r4, r3, r2, r1, r0 = forward(at, activations, act_peer, w_own, w_peer)
    got = shift(r4).astype(F32)
    got = shift(jnp.concatenate([r3[:32] + got, r3[32:]], 0).astype(BF16)).astype(F32)
    got = shift((r2 + got).astype(BF16)).astype(F32)
    got = shift((r1 + got).astype(BF16))
    summed = r0 + got[:32].astype(F32) + swap(got[32:]).astype(F32)
    output = (summed * col_scale).astype(BF16)

    at_peer = act_peer.T
    scaled, slope = slopes(at, block, (hop1, hop2, hop3), hop4, crossed, col_scale, w_own, w_peer, at_own, at_peer)
    slope = exchange(slope, "y")
    act_own, act_send, low = backward(at, scaled, w_own, w_peer, at_own, at_peer, second, adapter_out)
    low = exchange(pack(slope, low), REPLICA)
    low = exchange(combine(at, low, second, col_norm, magnitude), REPLICA)
    act_add = swap(act_send)
    payload, in_own = finish(at, low, w_own, w_peer, adapter_out, col_norm, magnitude)
    last = swap(payload)
    grad_in = (in_own + last[:64, half:]).T
    grad_out, grad_mag = join(at, payload, last)
    grad_mag = grad_mag[0]
    grad_act = (act_own + act_add.astype(F32)).astype(BF16)
    return (output, grad_act, grad_in, grad_out, grad_mag)


def solution(mesh):
    grid = Mesh(mesh.devices.reshape(8, 4, 8, 2), ("z", "x", "y", "core"))
    every = ("z", "x", "y", "core")
    in_specs = (P(REPLICA, TENSOR), P(TENSOR, None), P(TENSOR, None), P(), P(), P(every, None))
    out_specs = (P(every, None), P(REPLICA, TENSOR), P(TENSOR, None), P(), P())
    return jax.shard_map(program, mesh=grid, in_specs=in_specs, out_specs=out_specs, check_vma=False)
```

```python
import jax
import jax.numpy as jnp
from jax import lax
from jax.experimental import pallas as pl
from jax.experimental.pallas import tpu as pltpu
from jax.sharding import Mesh, PartitionSpec as P


epsilon = 1e-06
F32, BF16 = jnp.float32, jnp.bfloat16
REPLICA = ("z", "x")
TENSOR = ("y", "core")
TILE = 512


def split(value):
    high = value.astype(BF16)
    return high, (value - high.astype(F32)).astype(BF16)


def contract(left, right, dims):
    return lax.dot_general(left, right, ((dims[:1], dims[1:]), ((), ())), preferred_element_type=F32)


def merge_kernel(at_ref, base_ref, wide_ref, pair_ref, out_ref, z_ref, low_ref, first_ref):
    step = pl.program_id(0)
    ah, al = split(out_ref[...])
    low = contract(wide_ref[...], jnp.concatenate([ah, al, ah, al], 0), (1, 0))
    merged = base_ref[...].astype(F32) + low
    squares = jnp.sum(merged * merged, axis=0, keepdims=True)
    low_ref[...] = merged.astype(BF16)
    ranks = z_ref[pl.ds(pl.multiple_of(step * 16, 16), 16), :] + z_ref[pl.ds(pl.multiple_of(64 + step * 16, 16), 16), :]
    for k in range(4):
        member = 4 * step + k
        for q in range(4):
            first_ref[member, 4 * q : 4 * q + 4, :] = ranks[4 * k : 4 * k + 4, 128 * q : 128 * q + 128]
        for r in range(2):
            first_ref[member, 16 + r : 17 + r, :] = squares[:, 256 * k + 128 * r : 256 * k + 128 * r + 128]
        first_ref[member, 22:24, :] = jnp.zeros((2, 128), F32)

    @pl.when(lax.rem(step, 2) == at_ref[25])
    def _():
        span = pl.ds(pl.multiple_of(at_ref[26] * 128, 128), 128)
        rows = [pair_ref[pl.ds(pl.multiple_of(64 * k + at_ref[28] * 32, 32), 32), :] for k in range(2)]
        both = contract(jnp.concatenate(rows, 0), low_ref[:, span], (1, 0))
        block = both[:32] + both[32:]
        for k in range(8):
            first_ref[2 * k + step // 2, 18:22, :] = block[4 * k : 4 * k + 4]


def merge(at, base, wide, pair, adapter_out, z):
    rows, cols = base.shape
    tokens = z.shape[1]
    steps = cols // 1024
    tile = lambda i, c: (0, i)
    whole = lambda i, c: (0, 0)
    return pl.pallas_call(
        merge_kernel,
        out_shape=(jax.ShapeDtypeStruct((rows, cols), BF16), jax.ShapeDtypeStruct((16, 24, 128), F32)),
        grid_spec=pltpu.PrefetchScalarGridSpec(
            num_scalar_prefetch=1,
            grid=(steps,),
            in_specs=[
                pl.BlockSpec((rows, 1024), tile),
                pl.BlockSpec((rows, 256), whole),
                pl.BlockSpec((128, rows), whole),
                pl.BlockSpec((64, 1024), tile),
                pl.BlockSpec((128, tokens), whole),
            ],
            out_specs=(
                pl.BlockSpec((rows, 1024), tile),
                pl.BlockSpec((16, 24, 128), lambda i, c: (0, 0, 0)),
            ),
        ),
        cost_estimate=pl.CostEstimate(flops=1400000000, bytes_accessed=7000000, transcendentals=0),
        name="merge",
    )(at, base, wide, pair, adapter_out, z)


def forward_kernel(at_ref, a_ref, b_ref, wa_ref, wb_ref, r4_ref, r3_ref, r2_ref, r1_ref, r0_ref, acts):
    @pl.when(pl.program_id(0) == 0)
    def _():
        for k in range(8):
            rows = pl.ds(pl.multiple_of(at_ref[17 + k] * 32, 32), 32)
            acts[32 * k : 32 * k + 32, :256] = a_ref[rows, :]
            acts[32 * k : 32 * k + 32, 256:] = b_ref[rows, :]

    part = contract(acts[...], jnp.concatenate([wa_ref[...], wb_ref[...]], 0), (1, 0))
    r4_ref[...] = part[0:32].astype(BF16)
    r3_ref[...] = part[32:96]
    r2_ref[...] = part[96:160]
    r1_ref[...] = part[160:224]
    r0_ref[...] = part[224:256]


def forward(at, act_own, act_peer, w_own, w_peer):
    tokens, feats = act_own.shape
    cols = w_own.shape[1]
    whole = pl.BlockSpec((tokens, feats), lambda i, c: (0, 0))
    tile = lambda rows: pl.BlockSpec((rows, 1024), lambda i, c: (0, i))
    rows = (32, 64, 64, 64, 32)
    kinds = (BF16, F32, F32, F32, F32)
    return pl.pallas_call(
        forward_kernel,
        out_shape=tuple(jax.ShapeDtypeStruct((r, cols), k) for r, k in zip(rows, kinds)),
        grid_spec=pltpu.PrefetchScalarGridSpec(
            num_scalar_prefetch=1,
            grid=(cols // 1024,),
            in_specs=[whole, whole, tile(feats), tile(feats)],
            out_specs=tuple(tile(r) for r in rows),
            scratch_shapes=[pltpu.VMEM((256, 512), BF16)],
        ),
        cost_estimate=pl.CostEstimate(flops=2 * tokens * feats * cols, bytes_accessed=5000000, transcendentals=0),
        name="forward",
    )(at, act_own, act_peer, w_own, w_peer)


def slope_kernel(
    at_ref, block_ref, hop1_ref, hop2_ref, hop3_ref, hop4_ref, cross_ref, scale_ref, wo_ref, wp_ref, ato_ref, atp_ref,
    scaled_ref, slope_ref, cots,
):
    parts = [block_ref, hop1_ref, hop2_ref, hop3_ref, hop4_ref]
    parts = [(part, r) for part in parts for r in (0, 32)] + [(cross_ref, r) for r in range(0, 192, 32)]
    for k, (part, r) in enumerate(parts):
        cots[pl.ds(pl.multiple_of(at_ref[1 + k] * 32, 32), 32), :] = part[r : r + 32, :]
    cot = cots[...]
    slope = jnp.sum(contract(ato_ref[...], cot, (1, 0)) * wo_ref[...].astype(F32), axis=0, keepdims=True)
    slope = slope + jnp.sum(contract(atp_ref[...], cot, (1, 0)) * wp_ref[...].astype(F32), axis=0, keepdims=True)
    scaled_ref[...] = (cot.astype(F32) * scale_ref[...]).astype(BF16)
    for q in range(8):
        row = slope[:, 128 * q : 128 * q + 128]
        for k in range(8):
            slope_ref[k, q : q + 1, :] = row


def slopes(at, block, hops, hop4, crossed, scale, w_own, w_peer, at_own, at_peer):
    cols = hop4.shape[1]
    feats, tokens = at_own.shape
    steps = cols // 1024
    whole = lambda i, c: (0, 0)
    tile = lambda i, c: (0, i)
    side = lambda i, c: (0, c[0] * steps + i)
    return pl.pallas_call(
        slope_kernel,
        out_shape=(jax.ShapeDtypeStruct((tokens, cols), BF16), jax.ShapeDtypeStruct((8, 16, 128), F32)),
        grid_spec=pltpu.PrefetchScalarGridSpec(
            num_scalar_prefetch=1,
            grid=(steps,),
            in_specs=[pl.BlockSpec((64, 1024), side)] * 4
            + [
                pl.BlockSpec((64, 1024), tile),
                pl.BlockSpec((192, 1024), tile),
                pl.BlockSpec((1, 1024), side),
                pl.BlockSpec((feats, 1024), side),
                pl.BlockSpec((feats, 1024), side),
                pl.BlockSpec((feats, tokens), whole),
                pl.BlockSpec((feats, tokens), whole),
            ],
            out_specs=(pl.BlockSpec((tokens, 1024), tile), pl.BlockSpec((8, 8, 128), lambda i, c: (0, i, 0))),
            scratch_shapes=[pltpu.VMEM((tokens, 1024), BF16)],
        ),
        cost_estimate=pl.CostEstimate(flops=2200000000, bytes_accessed=8000000, transcendentals=0),
        name="slopes",
    )(at, block, *hops, hop4, crossed, scale, w_own, w_peer, at_own, at_peer)


def backward_kernel(
    at_ref, scaled_ref, wo_ref, wp_ref, ato_ref, atp_ref, second_ref, out_ref,
    gao_ref, gap_ref, low_ref, sum_own, sum_peer, sum_y, zt,
):
    step = pl.program_id(0)

    @pl.when(step == 0)
    def _():
        for m in range(16):
            for q in range(4):
                zt[4 * m : 4 * m + 4, 128 * q : 128 * q + 128] = second_ref[m, 4 * q : 4 * q + 4, :]

    scaled = scaled_ref[...]
    both = contract(jnp.concatenate(split(zt[...]), 0), scaled, (1, 0))
    p = (both[:64] + both[64:]).astype(BF16)
    for q in range(4):
        for r in range(2):
            low_ref[8 * step + 2 * q + r, 0:32, :] = p[32 * r : 32 * r + 32, 128 * q : 128 * q + 128]
    own = contract(scaled, wo_ref[...], (1, 1))
    peer = contract(scaled, wp_ref[...], (1, 1))
    y = contract(scaled, jnp.concatenate(split(out_ref[...]), 0), (1, 1))

    @pl.when(step == 0)
    def _():
        sum_own[...] = own
        sum_peer[...] = peer
        sum_y[...] = y

    @pl.when(step > 0)
    def _():
        sum_own[...] += own
        sum_peer[...] += peer
        sum_y[...] += y

    @pl.when(step == pl.num_programs(0) - 1)
    def _():
        gao_ref[...] = sum_own[...]
        gap_ref[...] = sum_peer[...].astype(BF16)
        low_ref[:, 40:48, :] = jnp.zeros((32, 8, 128), BF16)
        pair = jnp.concatenate(split(sum_y[...]), 0)
        for k, ref in enumerate((ato_ref, atp_ref)):
            both = contract(jnp.concatenate([ref[...], ref[...]], 1), pair, (1, 0)).T
            both = (both[:64] + both[64:]).astype(BF16)
            for a in range(8):
                for q in range(2):
                    low_ref[4 * a + 2 * k + q, 32:40, :] = both[8 * a : 8 * a + 8, 128 * q : 128 * q + 128]


def backward(at, scaled, w_own, w_peer, at_own, at_peer, second, adapter_out):
    tokens, cols = scaled.shape
    feats = at_own.shape[0]
    steps = cols // TILE
    whole = lambda i, c: (0, 0)
    tile = lambda i, c: (0, i)
    side = lambda i, c: (0, c[0] * steps + i)
    return pl.pallas_call(
        backward_kernel,
        out_shape=(
            jax.ShapeDtypeStruct((tokens, feats), F32),
            jax.ShapeDtypeStruct((tokens, feats), BF16),
            jax.ShapeDtypeStruct((32, 48, 128), BF16),
        ),
        grid_spec=pltpu.PrefetchScalarGridSpec(
            num_scalar_prefetch=1,
            grid=(steps,),
            in_specs=[
                pl.BlockSpec((tokens, TILE), tile),
                pl.BlockSpec((feats, TILE), side),
                pl.BlockSpec((feats, TILE), side),
                pl.BlockSpec((feats, tokens), whole),
                pl.BlockSpec((feats, tokens), whole),
                pl.BlockSpec((16, 24, 128), lambda i, c: (0, 0, 0)),
                pl.BlockSpec((64, TILE), side),
            ],
            out_specs=(
                pl.BlockSpec((tokens, feats), whole),
                pl.BlockSpec((tokens, feats), whole),
                pl.BlockSpec((32, 48, 128), lambda i, c: (0, 0, 0)),
            ),
            scratch_shapes=[
                pltpu.VMEM((tokens, feats), F32),
                pltpu.VMEM((tokens, feats), F32),
                pltpu.VMEM((tokens, 128), F32),
                pltpu.VMEM((64, tokens), F32),
            ],
        ),
        cost_estimate=pl.CostEstimate(flops=3000000000, bytes_accessed=6000000, transcendentals=0),
        name="backward",
    )(at, scaled, w_own, w_peer, at_own, at_peer, second, adapter_out)


def pack_kernel(got_ref, low_ref, o_ref):
    slope = jnp.sum(got_ref[...], axis=0)
    high, low = split(slope)
    high, low = high.astype(F32), low.astype(F32)
    none = jnp.zeros((6, 128), F32)
    for k in range(16):
        rows = jnp.concatenate([high[k : k + 1], low[k : k + 1], none], 0).astype(BF16)
        o_ref[2 * k] = rows
        o_ref[2 * k + 1] = rows


def pack(got, low):
    return pl.pallas_call(
        pack_kernel,
        out_shape=jax.ShapeDtypeStruct(low.shape, BF16),
        grid=(1,),
        in_specs=[pl.BlockSpec(got.shape, lambda i: (0, 0, 0)), pl.BlockSpec(memory_space=pl.ANY)],
        out_specs=pl.BlockSpec((32, 8, 128), lambda i: (0, 5, 0)),
        input_output_aliases={1: 0},
        cost_estimate=pl.CostEstimate(flops=20000, bytes_accessed=130000, transcendentals=0),
        name="pack",
    )(got, low)


def combine_kernel(at_ref, got_ref, second_ref, norm_ref, size_ref, o_ref):
    total = jnp.sum(got_ref[...].astype(F32), axis=0)
    norm = norm_ref[...]
    mag = (total[40:41] + total[41:42]) / norm
    coeff = -mag * size_ref[...] / (norm * norm)
    q = jnp.concatenate([second_ref[2 * k + at_ref[0], 18:22, :] for k in range(8)], 0)
    high, low = split(mag)
    out = (total[0:32] + q * coeff).astype(BF16)
    o_ref[...] = jnp.broadcast_to(jnp.concatenate([out, total[32:40].astype(BF16), high, low, jnp.zeros((6, 128), BF16)], 0), o_ref.shape)


def combine(at, got, second, norm, size):
    column = pl.BlockSpec((1, 128), lambda i, c: (0, c[0] * 16 + c[27]))
    block = pl.BlockSpec(got.shape, lambda i, c: (0, 0, 0))
    return pl.pallas_call(
        combine_kernel,
        out_shape=jax.ShapeDtypeStruct(got.shape, BF16),
        grid_spec=pltpu.PrefetchScalarGridSpec(
            num_scalar_prefetch=1,
            grid=(1,),
            in_specs=[block, pl.BlockSpec((16, 24, 128), lambda i, c: (0, 0, 0)), column, column],
            out_specs=block,
        ),
        cost_estimate=pl.CostEstimate(flops=2000000, bytes_accessed=700000, transcendentals=0),
        name="combine",
    )(at, got, second, norm, size)


def finish_kernel(at_ref, got_ref, wo_ref, wp_ref, a_ref, norm_ref, size_ref, last_ref, own_ref, sum_own, sum_peer):
    step = pl.program_id(0)
    mags = []
    for q in range(8):
        j = 16 * step + 2 * q
        mags.append(got_ref[j, 40:41, :].astype(F32) + got_ref[j, 41:42, :].astype(F32))
        span = pl.ds(pl.multiple_of(step * 1024 + 128 * q, 128), 128)
        for r in range(2):
            last_ref[32 * r : 32 * r + 32, span] = got_ref[j + r, 0:32, :].astype(F32)
    mag = jnp.concatenate(mags, 1)
    last_ref[64:72, pl.ds(pl.multiple_of(step * 1024, 1024), 1024)] = jnp.broadcast_to(mag, (8, 1024))
    norm = norm_ref[...]
    coeff = -mag * size_ref[...] / (norm * norm)
    pair = jnp.concatenate(split(a_ref[...] * coeff), 0)
    own = contract(wo_ref[...], pair, (1, 1))
    peer = contract(wp_ref[...], pair, (1, 1))

    @pl.when(step == 0)
    def _():
        sum_own[...] = own
        sum_peer[...] = peer

    @pl.when(step > 0)
    def _():
        own_total, peer_total = (sum_own[...] + own).T, (sum_peer[...] + peer).T
        own_ref[...] = own_total[:64] + own_total[64:]
        last_ref[0:64, 2048:2304] = peer_total[:64] + peer_total[64:]
        last_ref[64:72, 2048:2304] = jnp.zeros((8, 256), F32)
        for a in range(8):
            rows = slice(8 * a, 8 * a + 8)
            for q in range(2):
                span = slice(128 * q, 128 * q + 128)
                own_ref[rows, span] += got_ref[4 * a + q, 32:40, :].astype(F32)
                last_ref[rows, 2048 + 128 * q : 2176 + 128 * q] += got_ref[4 * a + 2 + q, 32:40, :].astype(F32)


def finish(at, got, w_own, w_peer, adapter_out, norm, size):
    side = lambda i, c: (0, c[0] * 2 + i)
    whole = lambda i, c: (0, 0)
    return pl.pallas_call(
        finish_kernel,
        out_shape=(jax.ShapeDtypeStruct((72, 2304), F32), jax.ShapeDtypeStruct((64, 256), F32)),
        grid_spec=pltpu.PrefetchScalarGridSpec(
            num_scalar_prefetch=1,
            grid=(2,),
            in_specs=[
                pl.BlockSpec(got.shape, lambda i, c: (0, 0, 0)),
                pl.BlockSpec((256, 1024), side),
                pl.BlockSpec((256, 1024), side),
                pl.BlockSpec((64, 1024), side),
                pl.BlockSpec((1, 1024), side),
                pl.BlockSpec((1, 1024), side),
            ],
            out_specs=(pl.BlockSpec((72, 2304), whole), pl.BlockSpec((64, 256), whole)),
            scratch_shapes=[pltpu.VMEM((256, 128), F32), pltpu.VMEM((256, 128), F32)],
        ),
        cost_estimate=pl.CostEstimate(flops=600000000, bytes_accessed=3000000, transcendentals=0),
        name="finish",
    )(at, got, w_own, w_peer, adapter_out, norm, size)


def join_kernel(at_ref, mine_ref, other_ref, own_ref, out_ref, mag_ref, in_ref):
    cols = out_ref.shape[1] // 2
    for ref, side in ((mine_ref, at_ref[0]), (other_ref, 1 - at_ref[0])):
        span = pl.ds(pl.multiple_of(side * cols, cols), cols)
        out_ref[:, span] = ref[0:64, 0:cols]
        mag_ref[:, span] = ref[64:65, 0:cols]
    in_ref[...] = (own_ref[...] + other_ref[0:64, cols:]).T


def join(at, mine, other, own):
    block = pl.BlockSpec(mine.shape, lambda i, c: (0, 0))
    shapes = ((64, 4096), (1, 4096), (256, 64))
    return pl.pallas_call(
        join_kernel,
        out_shape=tuple(jax.ShapeDtypeStruct(s, F32) for s in shapes),
        grid_spec=pltpu.PrefetchScalarGridSpec(
            num_scalar_prefetch=1,
            grid=(1,),
            in_specs=[block, block, pl.BlockSpec(own.shape, lambda i, c: (0, 0))],
            out_specs=tuple(pl.BlockSpec(s, lambda i, c: (0, 0)) for s in shapes),
        ),
        cost_estimate=pl.CostEstimate(flops=100000, bytes_accessed=2500000, transcendentals=0),
        name="join",
    )(at, mine, other, own)


def program(activations, base_weight, adapter_in, adapter_out, magnitude, cotangent):
    core = lax.axis_index("core")
    y = lax.axis_index("y")
    replica = lax.axis_index(REPLICA)
    sides = lax.axis_size("y")
    half = adapter_out.shape[1] // 2
    hops = [(2 * s, 2 * ((s + 1) % sides)) for s in range(sides)]
    hops += [(2 * s + 1, 2 * ((s - 1) % sides) + 1) for s in range(sides)]

    def swap(value):
        return lax.ppermute(value, "core", [(0, 1), (1, 0)])

    def shift(value):
        return lax.ppermute(value, TENSOR, hops)

    def exchange(value, axes):
        return lax.all_to_all(value, axes, 0, 0)

    def spread(value, axes):
        return exchange(jnp.broadcast_to(value, (lax.axis_size(axes),) + value.shape), axes)

    mine = lambda value: lax.dynamic_slice_in_dim(value, core * half, half, 1)
    other = lambda value: lax.dynamic_slice_in_dim(value, (1 - core) * half, half, 1)

    block = jnp.concatenate([cotangent, swap(cotangent)], 0)
    hop1 = shift(block)
    hop2 = shift(hop1)
    hop3 = shift(hop2)
    sign = 1 - 2 * core
    near, far = [], []
    for k in range(5):
        chip = lax.rem(y - sign * k + sides, sides) * 2
        near += [chip + core, chip + 1 - core]
    for k in range(1, 4):
        chip = lax.rem(y + sign * k + sides, sides) * 2
        far += [chip + 1 - core, chip + core]
    rows = [lax.rem(y + sign * 4 + sides, sides) * 2 + core]
    for k in (3, 2, 1):
        chip = lax.rem(y + sign * k + sides, sides) * 2
        rows += [chip + core, chip + 1 - core]
    rows += [2 * y + core]
    window, part = replica // 2, lax.rem(replica, 2)
    at = [core] + near + far + rows + [window // 8, lax.rem(window, 8), window, part]
    at = jnp.stack(at).astype(jnp.int32)

    at_own = activations.T
    at_peer = swap(at_own)
    high = lax.reduce_precision(adapter_in, 8, 7)
    rest = (adapter_in - high).astype(BF16)
    high = high.astype(BF16)
    wide = jnp.concatenate([high, high, rest, rest], 1)
    pair = jnp.concatenate([high.T, rest.T], 0)
    z = contract(pair, activations, (1, 1))
    w_own, first = merge(at, base_weight, wide, pair, adapter_out, z)
    w_peer = swap(w_own)
    first = jnp.sum(exchange(first, TENSOR), axis=0)
    second = spread(first, TENSOR)
    hop4 = shift(mine(hop3))
    crossed = swap(jnp.concatenate([other(hop1), other(hop2), other(hop3)], 0))

    square_sum = second[:, 16:18].reshape(1, 2 * half)
    magnitude = magnitude.reshape(1, 2 * half)
    col_scale = magnitude / jnp.sqrt(square_sum + epsilon)
    scaled, slope = slopes(at, block, (hop1, hop2, hop3), hop4, crossed, col_scale, w_own, w_peer, at_own, at_peer)
    turned, slope = lax.optimization_barrier((at_peer, slope))
    r4, r3, r2, r1, r0 = forward(at, activations, turned.T, w_own, w_peer)
    got = shift(r4).astype(F32)
    got = shift(jnp.concatenate([r3[:32] + got, r3[32:]], 0).astype(BF16)).astype(F32)
    got = shift((r2 + got).astype(BF16)).astype(F32)
    got = shift((r1 + got).astype(BF16))
    summed = r0 + got[:32].astype(F32) + swap(got[32:]).astype(F32)
    output = (summed * col_scale).astype(BF16)

    slope = exchange(slope, "y")
    square_sum, slope = lax.optimization_barrier((square_sum, slope))
    col_norm = jnp.sqrt(square_sum + epsilon)
    act_own, act_send, low = backward(at, scaled, w_own, w_peer, at_own, at_peer, second, adapter_out)
    low = exchange(pack(slope, low), REPLICA)
    low = exchange(combine(at, low, second, col_norm, magnitude), REPLICA)
    act_add = swap(act_send)
    payload, in_own = finish(at, low, w_own, w_peer, adapter_out, col_norm, magnitude)
    last = swap(payload)
    grad_out, grad_mag, grad_in = join(at, payload, last, in_own)
    grad_mag = grad_mag.reshape(2 * half)
    grad_act = (act_own + act_add.astype(F32)).astype(BF16)
    return (output, grad_act, grad_in, grad_out, grad_mag)


def solution(mesh):
    grid = Mesh(mesh.devices.reshape(8, 4, 8, 2), ("z", "x", "y", "core"))
    every = ("z", "x", "y", "core")
    in_specs = (P(REPLICA, TENSOR), P(TENSOR, None), P(TENSOR, None), P(), P(), P(every, None))
    out_specs = (P(every, None), P(REPLICA, TENSOR), P(TENSOR, None), P(), P())
    return jax.shard_map(program, mesh=grid, in_specs=in_specs, out_specs=out_specs, check_vma=False)
```

```python
import jax
import jax.numpy as jnp
from jax import lax
from jax.experimental import pallas as pl
from jax.experimental.pallas import tpu as pltpu
from jax.sharding import Mesh, PartitionSpec as P


epsilon = 1e-06
F32, BF16 = jnp.float32, jnp.bfloat16
REPLICA = ("z", "x")
TENSOR = ("y", "core")
TILE = 512


def split(value):
    high = value.astype(BF16)
    return high, (value - high.astype(F32)).astype(BF16)


def contract(left, right, dims):
    return lax.dot_general(left, right, ((dims[:1], dims[1:]), ((), ())), preferred_element_type=F32)


def merge_kernel(at_ref, base_ref, wide_ref, pair_ref, out_ref, z_ref, low_ref, first_ref):
    step = pl.program_id(0)
    ah, al = split(out_ref[...])
    low = contract(wide_ref[...], jnp.concatenate([ah, al, ah, al], 0), (1, 0))
    merged = base_ref[...].astype(F32) + low
    squares = jnp.sum(merged * merged, axis=0, keepdims=True)
    low_ref[...] = merged.astype(BF16)
    ranks = z_ref[pl.ds(pl.multiple_of(step * 16, 16), 16), :] + z_ref[pl.ds(pl.multiple_of(64 + step * 16, 16), 16), :]
    for k in range(4):
        member = 4 * step + k
        for q in range(4):
            first_ref[member, 4 * q : 4 * q + 4, :] = ranks[4 * k : 4 * k + 4, 128 * q : 128 * q + 128]
        for r in range(2):
            first_ref[member, 16 + r : 17 + r, :] = squares[:, 256 * k + 128 * r : 256 * k + 128 * r + 128]
        first_ref[member, 22:24, :] = jnp.zeros((2, 128), F32)

    @pl.when(lax.rem(step, 2) == at_ref[25])
    def _():
        span = pl.ds(pl.multiple_of(at_ref[26] * 128, 128), 128)
        rows = [pair_ref[pl.ds(pl.multiple_of(64 * k + at_ref[28] * 32, 32), 32), :] for k in range(2)]
        both = contract(jnp.concatenate(rows, 0), low_ref[:, span], (1, 0))
        block = both[:32] + both[32:]
        for k in range(8):
            first_ref[2 * k + step // 2, 18:22, :] = block[4 * k : 4 * k + 4]


def merge(at, base, wide, pair, adapter_out, z):
    rows, cols = base.shape
    tokens = z.shape[1]
    steps = cols // 1024
    tile = lambda i, c: (0, i)
    whole = lambda i, c: (0, 0)
    return pl.pallas_call(
        merge_kernel,
        out_shape=(jax.ShapeDtypeStruct((rows, cols), BF16), jax.ShapeDtypeStruct((16, 24, 128), F32)),
        grid_spec=pltpu.PrefetchScalarGridSpec(
            num_scalar_prefetch=1,
            grid=(steps,),
            in_specs=[
                pl.BlockSpec((rows, 1024), tile),
                pl.BlockSpec((rows, 256), whole),
                pl.BlockSpec((128, rows), whole),
                pl.BlockSpec((64, 1024), tile),
                pl.BlockSpec((128, tokens), whole),
            ],
            out_specs=(
                pl.BlockSpec((rows, 1024), tile),
                pl.BlockSpec((16, 24, 128), lambda i, c: (0, 0, 0)),
            ),
        ),
        cost_estimate=pl.CostEstimate(flops=1400000000, bytes_accessed=7000000, transcendentals=0),
        name="merge",
    )(at, base, wide, pair, adapter_out, z)


def forward_kernel(at_ref, a_ref, b_ref, wa_ref, wb_ref, *rest):
    refs, acts = rest[-7:-1], rest[-1]

    @pl.when(pl.program_id(0) == 0)
    def _():
        for k in range(8):
            rows = pl.ds(pl.multiple_of(at_ref[17 + k] * 32, 32), 32)
            acts[32 * k : 32 * k + 32, :256] = a_ref[rows, :]
            acts[32 * k : 32 * k + 32, 256:] = b_ref[rows, :]

    part = contract(acts[...], jnp.concatenate([wa_ref[...], wb_ref[...]], 0), (1, 0))
    refs[0][...] = part[0:32].astype(BF16)
    for ref, low, high in zip(refs[1:], (32, 64, 96, 160, 224), (64, 96, 160, 224, 256)):
        ref[...] = part[low:high]


def forward(at, act_own, act_peer, w_own, w_peer, begin, held=()):
    tokens, feats = act_own.shape
    cols = w_own.shape[1]
    steps = cols // 2048
    whole = pl.BlockSpec((tokens, feats), lambda i, c: (0, 0))
    tile = lambda rows: pl.BlockSpec((rows, 1024), lambda i, c: (0, i + begin))
    rows = (32, 32, 32, 64, 64, 32)
    kinds = (BF16, F32, F32, F32, F32, F32)
    return pl.pallas_call(
        forward_kernel,
        out_shape=tuple(jax.ShapeDtypeStruct((r, cols), k) for r, k in zip(rows, kinds)),
        grid_spec=pltpu.PrefetchScalarGridSpec(
            num_scalar_prefetch=1,
            grid=(steps,),
            in_specs=[whole, whole, tile(feats), tile(feats)] + [pl.BlockSpec(memory_space=pl.ANY)] * len(held),
            out_specs=tuple(tile(r) for r in rows),
            scratch_shapes=[pltpu.VMEM((256, 512), BF16)],
        ),
        input_output_aliases={5 + k: k for k in range(len(held))},
        cost_estimate=pl.CostEstimate(flops=tokens * feats * cols, bytes_accessed=4000000, transcendentals=0),
    )(at, act_own, act_peer, w_own, w_peer, *held)


def slope_kernel(
    at_ref, block_ref, hop1_ref, hop2_ref, hop3_ref, hop4_ref, cross_ref, scale_ref, wo_ref, wp_ref, ato_ref, atp_ref,
    scaled_ref, slope_ref, cots,
):
    parts = [block_ref, hop1_ref, hop2_ref, hop3_ref, hop4_ref]
    parts = [(part, r) for part in parts for r in (0, 32)] + [(cross_ref, r) for r in range(0, 192, 32)]
    for k, (part, r) in enumerate(parts):
        cots[pl.ds(pl.multiple_of(at_ref[1 + k] * 32, 32), 32), :] = part[r : r + 32, :]
    cot = cots[...]
    slope = jnp.sum(contract(ato_ref[...], cot, (1, 0)) * wo_ref[...].astype(F32), axis=0, keepdims=True)
    slope = slope + jnp.sum(contract(atp_ref[...], cot, (1, 0)) * wp_ref[...].astype(F32), axis=0, keepdims=True)
    scaled_ref[...] = (cot.astype(F32) * scale_ref[...]).astype(BF16)
    for q in range(8):
        row = slope[:, 128 * q : 128 * q + 128]
        for k in range(8):
            slope_ref[k, q : q + 1, :] = row


def slopes(at, block, hops, hop4, crossed, scale, w_own, w_peer, at_own, at_peer):
    cols = hop4.shape[1]
    feats, tokens = at_own.shape
    steps = cols // 1024
    whole = lambda i, c: (0, 0)
    tile = lambda i, c: (0, i)
    side = lambda i, c: (0, c[0] * steps + i)
    return pl.pallas_call(
        slope_kernel,
        out_shape=(jax.ShapeDtypeStruct((tokens, cols), BF16), jax.ShapeDtypeStruct((8, 16, 128), F32)),
        grid_spec=pltpu.PrefetchScalarGridSpec(
            num_scalar_prefetch=1,
            grid=(steps,),
            in_specs=[pl.BlockSpec((64, 1024), side)] * 4
            + [
                pl.BlockSpec((64, 1024), tile),
                pl.BlockSpec((192, 1024), tile),
                pl.BlockSpec((1, 1024), side),
                pl.BlockSpec((feats, 1024), side),
                pl.BlockSpec((feats, 1024), side),
                pl.BlockSpec((feats, tokens), whole),
                pl.BlockSpec((feats, tokens), whole),
            ],
            out_specs=(pl.BlockSpec((tokens, 1024), tile), pl.BlockSpec((8, 8, 128), lambda i, c: (0, i, 0))),
            scratch_shapes=[pltpu.VMEM((tokens, 1024), BF16)],
        ),
        cost_estimate=pl.CostEstimate(flops=2200000000, bytes_accessed=8000000, transcendentals=0),
        name="slopes",
    )(at, block, *hops, hop4, crossed, scale, w_own, w_peer, at_own, at_peer)


def backward_kernel(
    at_ref, scaled_ref, wo_ref, wp_ref, ato_ref, atp_ref, second_ref, out_ref,
    gao_ref, gap_ref, low_ref, sum_own, sum_peer, sum_y, zt,
):
    step = pl.program_id(0)

    @pl.when(step == 0)
    def _():
        for m in range(16):
            for q in range(4):
                zt[4 * m : 4 * m + 4, 128 * q : 128 * q + 128] = second_ref[m, 4 * q : 4 * q + 4, :]

    scaled = scaled_ref[...]
    both = contract(jnp.concatenate(split(zt[...]), 0), scaled, (1, 0))
    p = (both[:64] + both[64:]).astype(BF16)
    for q in range(4):
        for r in range(2):
            low_ref[8 * step + 2 * q + r, 0:32, :] = p[32 * r : 32 * r + 32, 128 * q : 128 * q + 128]
    own = contract(scaled, wo_ref[...], (1, 1))
    peer = contract(scaled, wp_ref[...], (1, 1))
    y = contract(scaled, jnp.concatenate(split(out_ref[...]), 0), (1, 1))

    @pl.when(step == 0)
    def _():
        sum_own[...] = own
        sum_peer[...] = peer
        sum_y[...] = y

    @pl.when(step > 0)
    def _():
        sum_own[...] += own
        sum_peer[...] += peer
        sum_y[...] += y

    @pl.when(step == pl.num_programs(0) - 1)
    def _():
        gao_ref[...] = sum_own[...]
        gap_ref[...] = sum_peer[...].astype(BF16)
        low_ref[:, 40:48, :] = jnp.zeros((32, 8, 128), BF16)
        pair = jnp.concatenate(split(sum_y[...]), 0)
        for k, ref in enumerate((ato_ref, atp_ref)):
            both = contract(jnp.concatenate([ref[...], ref[...]], 1), pair, (1, 0)).T
            both = (both[:64] + both[64:]).astype(BF16)
            for a in range(8):
                for q in range(2):
                    low_ref[4 * a + 2 * k + q, 32:40, :] = both[8 * a : 8 * a + 8, 128 * q : 128 * q + 128]


def backward(at, scaled, w_own, w_peer, at_own, at_peer, second, adapter_out):
    tokens, cols = scaled.shape
    feats = at_own.shape[0]
    steps = cols // TILE
    whole = lambda i, c: (0, 0)
    tile = lambda i, c: (0, i)
    side = lambda i, c: (0, c[0] * steps + i)
    return pl.pallas_call(
        backward_kernel,
        out_shape=(
            jax.ShapeDtypeStruct((tokens, feats), F32),
            jax.ShapeDtypeStruct((tokens, feats), BF16),
            jax.ShapeDtypeStruct((32, 48, 128), BF16),
        ),
        grid_spec=pltpu.PrefetchScalarGridSpec(
            num_scalar_prefetch=1,
            grid=(steps,),
            in_specs=[
                pl.BlockSpec((tokens, TILE), tile),
                pl.BlockSpec((feats, TILE), side),
                pl.BlockSpec((feats, TILE), side),
                pl.BlockSpec((feats, tokens), whole),
                pl.BlockSpec((feats, tokens), whole),
                pl.BlockSpec((16, 24, 128), lambda i, c: (0, 0, 0)),
                pl.BlockSpec((64, TILE), side),
            ],
            out_specs=(
                pl.BlockSpec((tokens, feats), whole),
                pl.BlockSpec((tokens, feats), whole),
                pl.BlockSpec((32, 48, 128), lambda i, c: (0, 0, 0)),
            ),
            scratch_shapes=[
                pltpu.VMEM((tokens, feats), F32),
                pltpu.VMEM((tokens, feats), F32),
                pltpu.VMEM((tokens, 128), F32),
                pltpu.VMEM((64, tokens), F32),
            ],
        ),
        cost_estimate=pl.CostEstimate(flops=3000000000, bytes_accessed=6000000, transcendentals=0),
        name="backward",
    )(at, scaled, w_own, w_peer, at_own, at_peer, second, adapter_out)


def pack_kernel(got_ref, low_ref, o_ref):
    slope = jnp.sum(got_ref[...], axis=0)
    high, low = split(slope)
    high, low = high.astype(F32), low.astype(F32)
    none = jnp.zeros((6, 128), F32)
    for k in range(16):
        rows = jnp.concatenate([high[k : k + 1], low[k : k + 1], none], 0).astype(BF16)
        o_ref[2 * k] = rows
        o_ref[2 * k + 1] = rows


def pack(got, low):
    return pl.pallas_call(
        pack_kernel,
        out_shape=jax.ShapeDtypeStruct(low.shape, BF16),
        grid=(1,),
        in_specs=[pl.BlockSpec(got.shape, lambda i: (0, 0, 0)), pl.BlockSpec(memory_space=pl.ANY)],
        out_specs=pl.BlockSpec((32, 8, 128), lambda i: (0, 5, 0)),
        input_output_aliases={1: 0},
        cost_estimate=pl.CostEstimate(flops=20000, bytes_accessed=130000, transcendentals=0),
        name="pack",
    )(got, low)


def combine_kernel(at_ref, got_ref, second_ref, norm_ref, size_ref, o_ref):
    total = jnp.sum(got_ref[...].astype(F32), axis=0)
    norm = norm_ref[...]
    mag = (total[40:41] + total[41:42]) / norm
    coeff = -mag * size_ref[...] / (norm * norm)
    q = jnp.concatenate([second_ref[2 * k + at_ref[0], 18:22, :] for k in range(8)], 0)
    high, low = split(mag)
    out = (total[0:32] + q * coeff).astype(BF16)
    o_ref[...] = jnp.broadcast_to(jnp.concatenate([out, total[32:40].astype(BF16), high, low, jnp.zeros((6, 128), BF16)], 0), o_ref.shape)


def combine(at, got, second, norm, size):
    column = pl.BlockSpec((1, 128), lambda i, c: (0, c[0] * 16 + c[27]))
    block = pl.BlockSpec(got.shape, lambda i, c: (0, 0, 0))
    return pl.pallas_call(
        combine_kernel,
        out_shape=jax.ShapeDtypeStruct(got.shape, BF16),
        grid_spec=pltpu.PrefetchScalarGridSpec(
            num_scalar_prefetch=1,
            grid=(1,),
            in_specs=[block, pl.BlockSpec((16, 24, 128), lambda i, c: (0, 0, 0)), column, column],
            out_specs=block,
        ),
        cost_estimate=pl.CostEstimate(flops=2000000, bytes_accessed=700000, transcendentals=0),
        name="combine",
    )(at, got, second, norm, size)


def finish_kernel(at_ref, got_ref, wo_ref, wp_ref, a_ref, norm_ref, size_ref, last_ref, own_ref, sum_own, sum_peer):
    step = pl.program_id(0)
    mags = []
    for q in range(8):
        j = 16 * step + 2 * q
        mags.append(got_ref[j, 40:41, :].astype(F32) + got_ref[j, 41:42, :].astype(F32))
        span = pl.ds(pl.multiple_of(step * 1024 + 128 * q, 128), 128)
        for r in range(2):
            last_ref[32 * r : 32 * r + 32, span] = got_ref[j + r, 0:32, :].astype(F32)
    mag = jnp.concatenate(mags, 1)
    last_ref[64:72, pl.ds(pl.multiple_of(step * 1024, 1024), 1024)] = jnp.broadcast_to(mag, (8, 1024))
    norm = norm_ref[...]
    coeff = -mag * size_ref[...] / (norm * norm)
    pair = jnp.concatenate(split(a_ref[...] * coeff), 0)
    own = contract(wo_ref[...], pair, (1, 1))
    peer = contract(wp_ref[...], pair, (1, 1))

    @pl.when(step == 0)
    def _():
        sum_own[...] = own
        sum_peer[...] = peer

    @pl.when(step > 0)
    def _():
        own_total, peer_total = (sum_own[...] + own).T, (sum_peer[...] + peer).T
        own_ref[...] = own_total[:64] + own_total[64:]
        last_ref[0:64, 2048:2304] = peer_total[:64] + peer_total[64:]
        last_ref[64:72, 2048:2304] = jnp.zeros((8, 256), F32)
        for a in range(8):
            rows = slice(8 * a, 8 * a + 8)
            for q in range(2):
                span = slice(128 * q, 128 * q + 128)
                own_ref[rows, span] += got_ref[4 * a + q, 32:40, :].astype(F32)
                last_ref[rows, 2048 + 128 * q : 2176 + 128 * q] += got_ref[4 * a + 2 + q, 32:40, :].astype(F32)


def finish(at, got, w_own, w_peer, adapter_out, norm, size):
    side = lambda i, c: (0, c[0] * 2 + i)
    whole = lambda i, c: (0, 0)
    return pl.pallas_call(
        finish_kernel,
        out_shape=(jax.ShapeDtypeStruct((72, 2304), F32), jax.ShapeDtypeStruct((64, 256), F32)),
        grid_spec=pltpu.PrefetchScalarGridSpec(
            num_scalar_prefetch=1,
            grid=(2,),
            in_specs=[
                pl.BlockSpec(got.shape, lambda i, c: (0, 0, 0)),
                pl.BlockSpec((256, 1024), side),
                pl.BlockSpec((256, 1024), side),
                pl.BlockSpec((64, 1024), side),
                pl.BlockSpec((1, 1024), side),
                pl.BlockSpec((1, 1024), side),
            ],
            out_specs=(pl.BlockSpec((72, 2304), whole), pl.BlockSpec((64, 256), whole)),
            scratch_shapes=[pltpu.VMEM((256, 128), F32), pltpu.VMEM((256, 128), F32)],
        ),
        cost_estimate=pl.CostEstimate(flops=600000000, bytes_accessed=3000000, transcendentals=0),
        name="finish",
    )(at, got, w_own, w_peer, adapter_out, norm, size)


def join_kernel(at_ref, mine_ref, other_ref, own_ref, out_ref, mag_ref, in_ref):
    cols = out_ref.shape[1] // 2
    for ref, side in ((mine_ref, at_ref[0]), (other_ref, 1 - at_ref[0])):
        span = pl.ds(pl.multiple_of(side * cols, cols), cols)
        out_ref[:, span] = ref[0:64, 0:cols]
        mag_ref[:, span] = ref[64:65, 0:cols]
    in_ref[...] = own_ref[...] + other_ref[0:64, cols:]


def join(at, mine, other, own):
    block = pl.BlockSpec(mine.shape, lambda i, c: (0, 0))
    shapes = ((64, 4096), (1, 4096), own.shape)
    return pl.pallas_call(
        join_kernel,
        out_shape=tuple(jax.ShapeDtypeStruct(s, F32) for s in shapes),
        grid_spec=pltpu.PrefetchScalarGridSpec(
            num_scalar_prefetch=1,
            grid=(1,),
            in_specs=[block, block, pl.BlockSpec(own.shape, lambda i, c: (0, 0))],
            out_specs=tuple(pl.BlockSpec(s, lambda i, c: (0, 0)) for s in shapes),
        ),
        cost_estimate=pl.CostEstimate(flops=100000, bytes_accessed=2500000, transcendentals=0),
        name="join",
    )(at, mine, other, own)


def program(activations, base_weight, adapter_in, adapter_out, magnitude, cotangent):
    core = lax.axis_index("core")
    y = lax.axis_index("y")
    replica = lax.axis_index(REPLICA)
    sides = lax.axis_size("y")
    half = adapter_out.shape[1] // 2
    hops = [(2 * s, 2 * ((s + 1) % sides)) for s in range(sides)]
    hops += [(2 * s + 1, 2 * ((s - 1) % sides) + 1) for s in range(sides)]

    def swap(value):
        return lax.ppermute(value, "core", [(0, 1), (1, 0)])

    def shift(value):
        return lax.ppermute(value, TENSOR, hops)

    def exchange(value, axes):
        return lax.all_to_all(value, axes, 0, 0)

    def spread(value, axes):
        return exchange(jnp.broadcast_to(value, (lax.axis_size(axes),) + value.shape), axes)

    mine = lambda value: lax.dynamic_slice_in_dim(value, core * half, half, 1)
    other = lambda value: lax.dynamic_slice_in_dim(value, (1 - core) * half, half, 1)

    block = jnp.concatenate([cotangent, swap(cotangent)], 0)
    hop1 = shift(block)
    hop2 = shift(hop1)
    hop3 = shift(hop2)
    sign = 1 - 2 * core
    near, far = [], []
    for k in range(5):
        chip = lax.rem(y - sign * k + sides, sides) * 2
        near += [chip + core, chip + 1 - core]
    for k in range(1, 4):
        chip = lax.rem(y + sign * k + sides, sides) * 2
        far += [chip + 1 - core, chip + core]
    rows = [lax.rem(y + sign * 4 + sides, sides) * 2 + core]
    for k in (3, 2, 1):
        chip = lax.rem(y + sign * k + sides, sides) * 2
        rows += [chip + core, chip + 1 - core]
    rows += [2 * y + core]
    window, part = replica // 2, lax.rem(replica, 2)
    at = [core] + near + far + rows + [window // 8, lax.rem(window, 8), window, part]
    at = jnp.stack(at).astype(jnp.int32)

    adapter_in, block = lax.optimization_barrier((adapter_in, block))
    high = lax.reduce_precision(adapter_in, 8, 7)
    rest = (adapter_in - high).astype(BF16)
    high = high.astype(BF16)
    wide = jnp.concatenate([high, high, rest, rest], 1)
    pair = jnp.concatenate([high.T, rest.T], 0)
    z = contract(pair, activations, (1, 1))
    w_own, first = merge(at, base_weight, wide, pair, adapter_out, z)
    late, first = lax.optimization_barrier((activations, first))
    at_own = late.T
    at_peer = swap(at_own)
    w_peer = swap(w_own)
    first = jnp.sum(exchange(first, TENSOR), axis=0)
    second = spread(first, TENSOR)
    hop4 = shift(mine(hop3))
    crossed = swap(jnp.concatenate([other(hop1), other(hop2), other(hop3)], 0))

    square_sum = second[:, 16:18].reshape(1, 2 * half)
    magnitude = magnitude.reshape(1, 2 * half)
    col_scale = magnitude / jnp.sqrt(square_sum + epsilon)
    act_peer = at_peer.T
    held = forward(at, activations, act_peer, w_own, w_peer, 0)
    r4, r3a, r3b, r2, r1, r0 = forward(at, activations, act_peer, w_own, w_peer, 2, held)
    got = shift(r4).astype(F32)
    got = shift(jnp.concatenate([r3a + got, r3b], 0).astype(BF16)).astype(F32)
    got = shift((r2 + got).astype(BF16)).astype(F32)
    got = shift((r1 + got).astype(BF16))
    summed = r0 + got[:32].astype(F32) + swap(got[32:]).astype(F32)
    output = (summed * col_scale).astype(BF16)
    scaled, slope = slopes(at, block, (hop1, hop2, hop3), hop4, crossed, col_scale, w_own, w_peer, at_own, at_peer)
    slope = exchange(slope, "y")
    square_sum, slope = lax.optimization_barrier((square_sum, slope))
    col_norm = jnp.sqrt(square_sum + epsilon)
    act_own, act_send, low = backward(at, scaled, w_own, w_peer, at_own, at_peer, second, adapter_out)
    low = exchange(pack(slope, low), REPLICA)
    low = exchange(combine(at, low, second, col_norm, magnitude), REPLICA)
    act_add = swap(act_send)
    payload, in_own = finish(at, low, w_own, w_peer, adapter_out, col_norm, magnitude)
    last = swap(payload)
    grad_out, grad_mag, grad_in = join(at, payload, last, in_own)
    grad_mag, grad_in = grad_mag.reshape(2 * half), grad_in.T
    grad_act = (act_own + act_add.astype(F32)).astype(BF16)
    return (output, grad_act, grad_in, grad_out, grad_mag)


def solution(mesh):
    grid = Mesh(mesh.devices.reshape(8, 4, 8, 2), ("z", "x", "y", "core"))
    every = ("z", "x", "y", "core")
    in_specs = (P(REPLICA, TENSOR), P(TENSOR, None), P(TENSOR, None), P(), P(), P(every, None))
    out_specs = (P(every, None), P(REPLICA, TENSOR), P(TENSOR, None), P(), P())
    return jax.shard_map(program, mesh=grid, in_specs=in_specs, out_specs=out_specs, check_vma=False)
```

```python
import jax
import jax.numpy as jnp
from jax import lax
from jax.experimental import pallas as pl
from jax.experimental.pallas import tpu as pltpu
from jax.sharding import Mesh, PartitionSpec as P


epsilon = 1e-06
F32, BF16 = jnp.float32, jnp.bfloat16
REPLICA = ("z", "x")
TENSOR = ("y", "core")
TILE = 512


def split(value):
    high = value.astype(BF16)
    return high, (value - high.astype(F32)).astype(BF16)


def contract(left, right, dims):
    return lax.dot_general(left, right, ((dims[:1], dims[1:]), ((), ())), preferred_element_type=F32)


def merge_kernel(at_ref, base_ref, wide_ref, pair_ref, out_ref, z_ref, low_ref, first_ref):
    step = pl.program_id(0)
    ah, al = split(out_ref[...])
    low = contract(wide_ref[...], jnp.concatenate([ah, al, ah, al], 0), (1, 0))
    merged = base_ref[...].astype(F32) + low
    squares = jnp.sum(merged * merged, axis=0, keepdims=True)
    low_ref[...] = merged.astype(BF16)
    ranks = z_ref[pl.ds(pl.multiple_of(step * 16, 16), 16), :] + z_ref[pl.ds(pl.multiple_of(64 + step * 16, 16), 16), :]
    for k in range(4):
        member = 4 * step + k
        for q in range(4):
            first_ref[member, 4 * q : 4 * q + 4, :] = ranks[4 * k : 4 * k + 4, 128 * q : 128 * q + 128]
        for r in range(2):
            first_ref[member, 16 + r : 17 + r, :] = squares[:, 256 * k + 128 * r : 256 * k + 128 * r + 128]
        first_ref[member, 22:24, :] = jnp.zeros((2, 128), F32)

    @pl.when(lax.rem(step, 2) == at_ref[25])
    def _():
        span = pl.ds(pl.multiple_of(at_ref[26] * 128, 128), 128)
        rows = [pair_ref[pl.ds(pl.multiple_of(64 * k + at_ref[28] * 32, 32), 32), :] for k in range(2)]
        both = contract(jnp.concatenate(rows, 0), low_ref[:, span], (1, 0))
        block = both[:32] + both[32:]
        for k in range(8):
            first_ref[2 * k + step // 2, 18:22, :] = block[4 * k : 4 * k + 4]


def merge(at, base, wide, pair, adapter_out, z):
    rows, cols = base.shape
    tokens = z.shape[1]
    steps = cols // 1024
    tile = lambda i, c: (0, i)
    whole = lambda i, c: (0, 0)
    return pl.pallas_call(
        merge_kernel,
        out_shape=(jax.ShapeDtypeStruct((rows, cols), BF16), jax.ShapeDtypeStruct((16, 24, 128), F32)),
        grid_spec=pltpu.PrefetchScalarGridSpec(
            num_scalar_prefetch=1,
            grid=(steps,),
            in_specs=[
                pl.BlockSpec((rows, 1024), tile),
                pl.BlockSpec((rows, 256), whole),
                pl.BlockSpec((128, rows), whole),
                pl.BlockSpec((64, 1024), tile),
                pl.BlockSpec((128, tokens), whole),
            ],
            out_specs=(
                pl.BlockSpec((rows, 1024), tile),
                pl.BlockSpec((16, 24, 128), lambda i, c: (0, 0, 0)),
            ),
        ),
        cost_estimate=pl.CostEstimate(flops=1400000000, bytes_accessed=7000000, transcendentals=0),
        name="merge",
    )(at, base, wide, pair, adapter_out, z)


def forward_kernel(at_ref, a_ref, b_ref, wa_ref, wb_ref, r4_ref, r3_ref, r2_ref, r1_ref, r0_ref, acts):
    @pl.when(pl.program_id(0) == 0)
    def _():
        for k in range(8):
            rows = pl.ds(pl.multiple_of(at_ref[17 + k] * 32, 32), 32)
            acts[32 * k : 32 * k + 32, :256] = a_ref[rows, :]
            acts[32 * k : 32 * k + 32, 256:] = b_ref[rows, :]

    part = contract(acts[...], jnp.concatenate([wa_ref[...], wb_ref[...]], 0), (1, 0))
    r4_ref[...] = part[0:32].astype(BF16)
    r3_ref[...] = part[32:96].astype(BF16)
    r2_ref[...] = part[96:160]
    r1_ref[...] = part[160:224]
    r0_ref[...] = part[224:256]


def forward(at, act_own, act_peer, w_own, w_peer):
    tokens, feats = act_own.shape
    cols = w_own.shape[1]
    whole = pl.BlockSpec((tokens, feats), lambda i, c: (0, 0))
    tile = lambda rows: pl.BlockSpec((rows, 1024), lambda i, c: (0, i))
    rows = (32, 64, 64, 64, 32)
    kinds = (BF16, BF16, F32, F32, F32)
    return pl.pallas_call(
        forward_kernel,
        out_shape=tuple(jax.ShapeDtypeStruct((r, cols), k) for r, k in zip(rows, kinds)),
        grid_spec=pltpu.PrefetchScalarGridSpec(
            num_scalar_prefetch=1,
            grid=(cols // 1024,),
            in_specs=[whole, whole, tile(feats), tile(feats)],
            out_specs=tuple(tile(r) for r in rows),
            scratch_shapes=[pltpu.VMEM((256, 512), BF16)],
        ),
        cost_estimate=pl.CostEstimate(flops=2 * tokens * feats * cols, bytes_accessed=5000000, transcendentals=0),
        name="forward",
    )(at, act_own, act_peer, w_own, w_peer)


def slope_kernel(
    at_ref, block_ref, hop1_ref, hop2_ref, hop3_ref, hop4_ref, cross_ref, scale_ref, wo_ref, wp_ref, ato_ref, atp_ref,
    scaled_ref, slope_ref, cots,
):
    parts = [block_ref, hop1_ref, hop2_ref, hop3_ref, hop4_ref]
    parts = [(part, r) for part in parts for r in (0, 32)] + [(cross_ref, r) for r in range(0, 192, 32)]
    for k, (part, r) in enumerate(parts):
        cots[pl.ds(pl.multiple_of(at_ref[1 + k] * 32, 32), 32), :] = part[r : r + 32, :]
    cot = cots[...]
    weight = jnp.concatenate([wo_ref[...], wp_ref[...]], 0).astype(F32)
    slope = contract(jnp.concatenate([ato_ref[...], atp_ref[...]], 0), cot, (1, 0)) * weight
    slope = jnp.sum(slope, axis=0, keepdims=True)
    scaled_ref[...] = (cot.astype(F32) * scale_ref[...]).astype(BF16)
    for q in range(8):
        row = slope[:, 128 * q : 128 * q + 128]
        for k in range(8):
            slope_ref[k, q : q + 1, :] = row


def slopes(at, block, hops, hop4, crossed, scale, w_own, w_peer, at_own, at_peer):
    cols = hop4.shape[1]
    feats, tokens = at_own.shape
    steps = cols // 1024
    whole = lambda i, c: (0, 0)
    tile = lambda i, c: (0, i)
    side = lambda i, c: (0, c[0] * steps + i)
    return pl.pallas_call(
        slope_kernel,
        out_shape=(jax.ShapeDtypeStruct((tokens, cols), BF16), jax.ShapeDtypeStruct((8, 16, 128), F32)),
        grid_spec=pltpu.PrefetchScalarGridSpec(
            num_scalar_prefetch=1,
            grid=(steps,),
            in_specs=[pl.BlockSpec((64, 1024), side)] * 4
            + [
                pl.BlockSpec((64, 1024), tile),
                pl.BlockSpec((192, 1024), tile),
                pl.BlockSpec((1, 1024), side),
                pl.BlockSpec((feats, 1024), side),
                pl.BlockSpec((feats, 1024), side),
                pl.BlockSpec((feats, tokens), whole),
                pl.BlockSpec((feats, tokens), whole),
            ],
            out_specs=(pl.BlockSpec((tokens, 1024), tile), pl.BlockSpec((8, 8, 128), lambda i, c: (0, i, 0))),
            scratch_shapes=[pltpu.VMEM((tokens, 1024), BF16)],
        ),
        cost_estimate=pl.CostEstimate(flops=2200000000, bytes_accessed=8000000, transcendentals=0),
        name="slopes",
    )(at, block, *hops, hop4, crossed, scale, w_own, w_peer, at_own, at_peer)


def backward_kernel(
    at_ref, scaled_ref, wo_ref, wp_ref, ato_ref, atp_ref, second_ref, out_ref,
    gao_ref, gap_ref, low_ref, sum_own, sum_peer, sum_y, zt,
):
    step = pl.program_id(0)

    @pl.when(step == 0)
    def _():
        for m in range(16):
            for q in range(4):
                zt[4 * m : 4 * m + 4, 128 * q : 128 * q + 128] = second_ref[m, 4 * q : 4 * q + 4, :]

    scaled = scaled_ref[...]
    both = contract(jnp.concatenate(split(zt[...]), 0), scaled, (1, 0))
    p = (both[:64] + both[64:]).astype(BF16)
    for q in range(4):
        for r in range(2):
            low_ref[8 * step + 2 * q + r, 0:32, :] = p[32 * r : 32 * r + 32, 128 * q : 128 * q + 128]
    own = contract(scaled, wo_ref[...], (1, 1))
    peer = contract(scaled, wp_ref[...], (1, 1))
    y = contract(scaled, jnp.concatenate(split(out_ref[...]), 0), (1, 1))

    @pl.when(step == 0)
    def _():
        sum_own[...] = own
        sum_peer[...] = peer
        sum_y[...] = y

    @pl.when(step > 0)
    def _():
        sum_own[...] += own
        sum_peer[...] += peer
        sum_y[...] += y

    @pl.when(step == pl.num_programs(0) - 1)
    def _():
        gao_ref[...] = sum_own[...]
        gap_ref[...] = sum_peer[...].astype(BF16)
        low_ref[:, 40:48, :] = jnp.zeros((32, 8, 128), BF16)
        pair = jnp.concatenate(split(sum_y[...]), 0)
        for k, ref in enumerate((ato_ref, atp_ref)):
            both = contract(jnp.concatenate([ref[...], ref[...]], 1), pair, (1, 0)).T
            both = (both[:64] + both[64:]).astype(BF16)
            for a in range(8):
                for q in range(2):
                    low_ref[4 * a + 2 * k + q, 32:40, :] = both[8 * a : 8 * a + 8, 128 * q : 128 * q + 128]


def backward(at, scaled, w_own, w_peer, at_own, at_peer, second, adapter_out):
    tokens, cols = scaled.shape
    feats = at_own.shape[0]
    steps = cols // TILE
    whole = lambda i, c: (0, 0)
    tile = lambda i, c: (0, i)
    side = lambda i, c: (0, c[0] * steps + i)
    return pl.pallas_call(
        backward_kernel,
        out_shape=(
            jax.ShapeDtypeStruct((tokens, feats), F32),
            jax.ShapeDtypeStruct((tokens, feats), BF16),
            jax.ShapeDtypeStruct((32, 48, 128), BF16),
        ),
        grid_spec=pltpu.PrefetchScalarGridSpec(
            num_scalar_prefetch=1,
            grid=(steps,),
            in_specs=[
                pl.BlockSpec((tokens, TILE), tile),
                pl.BlockSpec((feats, TILE), side),
                pl.BlockSpec((feats, TILE), side),
                pl.BlockSpec((feats, tokens), whole),
                pl.BlockSpec((feats, tokens), whole),
                pl.BlockSpec((16, 24, 128), lambda i, c: (0, 0, 0)),
                pl.BlockSpec((64, TILE), side),
            ],
            out_specs=(
                pl.BlockSpec((tokens, feats), whole),
                pl.BlockSpec((tokens, feats), whole),
                pl.BlockSpec((32, 48, 128), lambda i, c: (0, 0, 0)),
            ),
            scratch_shapes=[
                pltpu.VMEM((tokens, feats), F32),
                pltpu.VMEM((tokens, feats), F32),
                pltpu.VMEM((tokens, 128), F32),
                pltpu.VMEM((64, tokens), F32),
            ],
        ),
        cost_estimate=pl.CostEstimate(flops=3000000000, bytes_accessed=6000000, transcendentals=0),
        name="backward",
    )(at, scaled, w_own, w_peer, at_own, at_peer, second, adapter_out)


def pack_kernel(got_ref, low_ref, o_ref):
    slope = jnp.sum(got_ref[...], axis=0)
    high, low = split(slope)
    high, low = high.astype(F32), low.astype(F32)
    none = jnp.zeros((6, 128), F32)
    for k in range(16):
        rows = jnp.concatenate([high[k : k + 1], low[k : k + 1], none], 0).astype(BF16)
        o_ref[2 * k] = rows
        o_ref[2 * k + 1] = rows


def pack(got, low):
    return pl.pallas_call(
        pack_kernel,
        out_shape=jax.ShapeDtypeStruct(low.shape, BF16),
        grid=(1,),
        in_specs=[pl.BlockSpec(got.shape, lambda i: (0, 0, 0)), pl.BlockSpec(memory_space=pl.ANY)],
        out_specs=pl.BlockSpec((32, 8, 128), lambda i: (0, 5, 0)),
        input_output_aliases={1: 0},
        cost_estimate=pl.CostEstimate(flops=20000, bytes_accessed=130000, transcendentals=0),
        name="pack",
    )(got, low)


def combine_kernel(at_ref, got_ref, second_ref, norm_ref, size_ref, o_ref):
    total = jnp.sum(got_ref[...].astype(F32), axis=0)
    norm = norm_ref[...]
    mag = (total[40:41] + total[41:42]) / norm
    coeff = -mag * size_ref[...] / (norm * norm)
    q = jnp.concatenate([second_ref[2 * k + at_ref[0], 18:22, :] for k in range(8)], 0)
    high, low = split(mag)
    out = (total[0:32] + q * coeff).astype(BF16)
    o_ref[...] = jnp.broadcast_to(jnp.concatenate([out, total[32:40].astype(BF16), high, low, jnp.zeros((6, 128), BF16)], 0), o_ref.shape)


def combine(at, got, second, norm, size):
    column = pl.BlockSpec((1, 128), lambda i, c: (0, c[0] * 16 + c[27]))
    block = pl.BlockSpec(got.shape, lambda i, c: (0, 0, 0))
    return pl.pallas_call(
        combine_kernel,
        out_shape=jax.ShapeDtypeStruct(got.shape, BF16),
        grid_spec=pltpu.PrefetchScalarGridSpec(
            num_scalar_prefetch=1,
            grid=(1,),
            in_specs=[block, pl.BlockSpec((16, 24, 128), lambda i, c: (0, 0, 0)), column, column],
            out_specs=block,
        ),
        cost_estimate=pl.CostEstimate(flops=2000000, bytes_accessed=700000, transcendentals=0),
        name="combine",
    )(at, got, second, norm, size)


def finish_kernel(at_ref, got_ref, wo_ref, wp_ref, a_ref, norm_ref, size_ref, last_ref, own_ref, sum_own, sum_peer):
    step = pl.program_id(0)
    mags = []
    for q in range(8):
        j = 16 * step + 2 * q
        mags.append(got_ref[j, 40:41, :].astype(F32) + got_ref[j, 41:42, :].astype(F32))
        span = pl.ds(pl.multiple_of(step * 1024 + 128 * q, 128), 128)
        for r in range(2):
            last_ref[32 * r : 32 * r + 32, span] = got_ref[j + r, 0:32, :].astype(F32)
    mag = jnp.concatenate(mags, 1)
    last_ref[64:72, pl.ds(pl.multiple_of(step * 1024, 1024), 1024)] = jnp.broadcast_to(mag, (8, 1024))
    norm = norm_ref[...]
    coeff = -mag * size_ref[...] / (norm * norm)
    pair = jnp.concatenate(split(a_ref[...] * coeff), 0)
    own = contract(wo_ref[...], pair, (1, 1))
    peer = contract(wp_ref[...], pair, (1, 1))

    @pl.when(step == 0)
    def _():
        sum_own[...] = own
        sum_peer[...] = peer

    @pl.when(step > 0)
    def _():
        own_total, peer_total = (sum_own[...] + own).T, (sum_peer[...] + peer).T
        own_ref[...] = own_total[:64] + own_total[64:]
        last_ref[0:64, 2048:2304] = peer_total[:64] + peer_total[64:]
        last_ref[64:72, 2048:2304] = jnp.zeros((8, 256), F32)
        for a in range(8):
            rows = slice(8 * a, 8 * a + 8)
            for q in range(2):
                span = slice(128 * q, 128 * q + 128)
                own_ref[rows, span] += got_ref[4 * a + q, 32:40, :].astype(F32)
                last_ref[rows, 2048 + 128 * q : 2176 + 128 * q] += got_ref[4 * a + 2 + q, 32:40, :].astype(F32)


def finish(at, got, w_own, w_peer, adapter_out, norm, size):
    side = lambda i, c: (0, c[0] * 2 + i)
    whole = lambda i, c: (0, 0)
    return pl.pallas_call(
        finish_kernel,
        out_shape=(jax.ShapeDtypeStruct((72, 2304), F32), jax.ShapeDtypeStruct((64, 256), F32)),
        grid_spec=pltpu.PrefetchScalarGridSpec(
            num_scalar_prefetch=1,
            grid=(2,),
            in_specs=[
                pl.BlockSpec(got.shape, lambda i, c: (0, 0, 0)),
                pl.BlockSpec((256, 1024), side),
                pl.BlockSpec((256, 1024), side),
                pl.BlockSpec((64, 1024), side),
                pl.BlockSpec((1, 1024), side),
                pl.BlockSpec((1, 1024), side),
            ],
            out_specs=(pl.BlockSpec((72, 2304), whole), pl.BlockSpec((64, 256), whole)),
            scratch_shapes=[pltpu.VMEM((256, 128), F32), pltpu.VMEM((256, 128), F32)],
        ),
        cost_estimate=pl.CostEstimate(flops=600000000, bytes_accessed=3000000, transcendentals=0),
        name="finish",
    )(at, got, w_own, w_peer, adapter_out, norm, size)


def join_kernel(at_ref, mine_ref, other_ref, own_ref, out_ref, mag_ref, in_ref):
    cols = out_ref.shape[1] // 2
    for ref, side in ((mine_ref, at_ref[0]), (other_ref, 1 - at_ref[0])):
        span = pl.ds(pl.multiple_of(side * cols, cols), cols)
        out_ref[:, span] = ref[0:64, 0:cols]
        mag_ref[:, span] = ref[64:65, 0:cols]
    in_ref[...] = own_ref[...] + other_ref[0:64, cols:]


def join(at, mine, other, own):
    block = pl.BlockSpec(mine.shape, lambda i, c: (0, 0))
    shapes = ((64, 4096), (1, 4096), own.shape)
    return pl.pallas_call(
        join_kernel,
        out_shape=tuple(jax.ShapeDtypeStruct(s, F32) for s in shapes),
        grid_spec=pltpu.PrefetchScalarGridSpec(
            num_scalar_prefetch=1,
            grid=(1,),
            in_specs=[block, block, pl.BlockSpec(own.shape, lambda i, c: (0, 0))],
            out_specs=tuple(pl.BlockSpec(s, lambda i, c: (0, 0)) for s in shapes),
        ),
        cost_estimate=pl.CostEstimate(flops=100000, bytes_accessed=2500000, transcendentals=0),
        name="join",
    )(at, mine, other, own)


def program(activations, base_weight, adapter_in, adapter_out, magnitude, cotangent):
    core = lax.axis_index("core")
    y = lax.axis_index("y")
    replica = lax.axis_index(REPLICA)
    sides = lax.axis_size("y")
    half = adapter_out.shape[1] // 2
    hops = [(2 * s, 2 * ((s + 1) % sides)) for s in range(sides)]
    hops += [(2 * s + 1, 2 * ((s - 1) % sides) + 1) for s in range(sides)]

    def swap(value):
        return lax.ppermute(value, "core", [(0, 1), (1, 0)])

    def shift(value):
        return lax.ppermute(value, TENSOR, hops)

    def exchange(value, axes):
        return lax.all_to_all(value, axes, 0, 0)

    def spread(value, axes):
        return exchange(jnp.broadcast_to(value, (lax.axis_size(axes),) + value.shape), axes)

    mine = lambda value: lax.dynamic_slice_in_dim(value, core * half, half, 1)
    other = lambda value: lax.dynamic_slice_in_dim(value, (1 - core) * half, half, 1)

    block = jnp.concatenate([cotangent, swap(cotangent)], 0)
    hop1 = shift(block)
    hop2 = shift(hop1)
    hop3 = shift(hop2)
    sign = 1 - 2 * core
    near, far = [], []
    for k in range(5):
        chip = lax.rem(y - sign * k + sides, sides) * 2
        near += [chip + core, chip + 1 - core]
    for k in range(1, 4):
        chip = lax.rem(y + sign * k + sides, sides) * 2
        far += [chip + 1 - core, chip + core]
    rows = [lax.rem(y + sign * 4 + sides, sides) * 2 + core]
    for k in (3, 2, 1):
        chip = lax.rem(y + sign * k + sides, sides) * 2
        rows += [chip + core, chip + 1 - core]
    rows += [2 * y + core]
    window, part = replica // 2, lax.rem(replica, 2)
    at = [core] + near + far + rows + [window // 8, lax.rem(window, 8), window, part]
    at = jnp.stack(at).astype(jnp.int32)

    adapter_in, block = lax.optimization_barrier((adapter_in, block))
    high = lax.reduce_precision(adapter_in, 8, 7)
    rest = (adapter_in - high).astype(BF16)
    high = high.astype(BF16)
    wide = jnp.concatenate([high, high, rest, rest], 1)
    pair = jnp.concatenate([high.T, rest.T], 0)
    z = contract(pair, activations, (1, 1))
    w_own, first = merge(at, base_weight, wide, pair, adapter_out, z)
    late, first = lax.optimization_barrier((activations, first))
    at_own = late.T
    at_peer = swap(at_own)
    w_peer = swap(w_own)
    first = jnp.sum(exchange(first, TENSOR), axis=0)
    second = spread(first, TENSOR)
    hop4 = shift(mine(hop3))
    crossed = swap(jnp.concatenate([other(hop1), other(hop2), other(hop3)], 0))

    square_sum = second[:, 16:18].reshape(1, 2 * half)
    magnitude = magnitude.reshape(1, 2 * half)
    col_scale = magnitude / jnp.sqrt(square_sum + epsilon)
    act_peer = at_peer.T
    r4, r3, r2, r1, r0 = forward(at, activations, act_peer, w_own, w_peer)
    got = shift(r3).astype(F32)
    got = shift((r2 + got).astype(BF16)).astype(F32)
    got = shift((r1 + got).astype(BF16))
    across = lax.ppermute(r4, "y", [(s, (s + sides // 2) % sides) for s in range(sides)])
    summed = r0 + across.astype(F32) + got[:32].astype(F32) + swap(got[32:]).astype(F32)
    output = (summed * col_scale).astype(BF16)
    scaled, slope = slopes(at, block, (hop1, hop2, hop3), hop4, crossed, col_scale, w_own, w_peer, at_own, at_peer)
    slope = exchange(slope, "y")
    square_sum, slope = lax.optimization_barrier((square_sum, slope))
    col_norm = jnp.sqrt(square_sum + epsilon)
    act_own, act_send, low = backward(at, scaled, w_own, w_peer, at_own, at_peer, second, adapter_out)
    low = exchange(pack(slope, low), REPLICA)
    low = exchange(combine(at, low, second, col_norm, magnitude), REPLICA)
    act_add = swap(act_send)
    payload, in_own = finish(at, low, w_own, w_peer, adapter_out, col_norm, magnitude)
    last = swap(payload)
    grad_out, grad_mag, grad_in = join(at, payload, last, in_own)
    grad_mag, grad_in = grad_mag.reshape(2 * half), grad_in.T
    grad_act = (act_own + act_add.astype(F32)).astype(BF16)
    return (output, grad_act, grad_in, grad_out, grad_mag)


def solution(mesh):
    grid = Mesh(mesh.devices.reshape(8, 4, 8, 2), ("z", "x", "y", "core"))
    every = ("z", "x", "y", "core")
    in_specs = (P(REPLICA, TENSOR), P(TENSOR, None), P(TENSOR, None), P(), P(), P(every, None))
    out_specs = (P(every, None), P(REPLICA, TENSOR), P(TENSOR, None), P(), P())
    return jax.shard_map(program, mesh=grid, in_specs=in_specs, out_specs=out_specs, check_vma=False)
```
